256 devices in a mesh: leaf: 32 (over z, y), front: 8 (over x, core).
Axes of the slice: x: 4, y: 4, z: 8, core: 2. Of those that a mesh axis runs over, the one named last changes fastest.
Arguments:
- leaf_fronts: float32 [32, 1, 2048, 2048], P('leaf', None, 'front'), may hold values from -40 to 40, as said below
- screen_weights: float32 [32, 1, 2048], P('leaf', None, 'front'), may hold values from 0.1 to 2
- parent_tile_index: int32 [32, 1, 12], replicated, may hold values from 0 to 31, as said below
Outputs:
- leaf_panel: float32 [32, 1, 2048, 512], P('leaf', None, 'front')
- parent_panel: float32 [32, 1, 2048, 128], P('leaf', None, 'front')
- parent_update: float32 [32, 1, 2048, 3968], P('leaf', None, 'front')
The draws below stay inside these ranges and needn't reach their ends.
Inputs may be any that keep to these rules, and one draw needn't show every extreme that they name: `leaf_fronts`: each first-level front is symmetric positive definite. `parent_tile_index`: entry [i, g, a] is the tile of parent (i // 2, g) that receives contribution tile t = 4 * (a // 3) + a % 3 + 1 of front (i, g); tile p covers rows p * 128 to (p + 1) * 128 - 1. The entries of one front are distinct, tile 1 always goes to parent tile 0, and p * 128 // 512 == t * 128 // 256.
All inputs are finite; a program needn't handle non-finite values.
Results may differ from the reference program's by a relative error of at most 0.00013.
Values sent between devices are 32-bit elements; how exact they have to be, the bound alone decides.
A program may use at most 128 MiB of HBM per device.

```python
import math
import jax
import jax.numpy as jnp
from jax import lax

SEPARATOR_ONE = 512
SEP2 = 1024
PANEL_WIDTH = 128
FRONTS_PER_LEVEL = 1
FRONT_ORDER_M1 = 2048
M2 = 4096
LEAVES = 32
ROWS1 = 256
ROWS2 = 256
FRONT_TILES_ONE = 16
ELIMINATED_TILES = 4
N_FRONT = 8


def draw_leaf_fronts(key, part):
    first, second, third = jax.random.split(key, 3)
    shape = (LEAVES, FRONTS_PER_LEVEL, FRONT_ORDER_M1, FRONT_ORDER_M1)
    raw = jnp.clip(jax.random.normal(first, shape, jnp.float32), -4.0, 4.0) * (1.15 / math.sqrt(FRONT_ORDER_M1))
    diagonal = 2.5 + jax.random.uniform(second, (LEAVES, FRONTS_PER_LEVEL, FRONT_ORDER_M1), jnp.float32)
    coupling = jnp.clip(jax.random.normal(third, (LEAVES, FRONTS_PER_LEVEL, FRONT_ORDER_M1, PANEL_WIDTH), jnp.float32), -4.0, 4.0)
    coupling = coupling * (1.5 / math.sqrt(PANEL_WIDTH))
    symmetric = 0.5 * (raw + jnp.swapaxes(raw, 2, 3))
    row_ids = lax.broadcasted_iota(jnp.int32, (1, 1, FRONT_ORDER_M1, FRONT_ORDER_M1), 2)
    col_ids = lax.broadcasted_iota(jnp.int32, (1, 1, FRONT_ORDER_M1, FRONT_ORDER_M1), 3)
    base = jnp.where(row_ids == col_ids, diagonal[:, :, :, None], symmetric)
    return base + jnp.einsum('lgnp,lgmp->lgnm', coupling, coupling, precision=lax.Precision.HIGHEST)


def draw_parent_tile_index(key, part):
    blocks = FRONT_ORDER_M1 // ROWS1
    count = ROWS1 // PANEL_WIDTH
    slots = 2 * count
    shape = (LEAVES, FRONTS_PER_LEVEL, blocks, slots)
    scores = jax.random.randint(key, shape, 0, 2 ** 24)
    slot_ids = lax.broadcasted_iota(jnp.int32, shape, 3)
    block_ids = lax.broadcasted_iota(jnp.int32, shape, 2)
    leaf_ids = lax.broadcasted_iota(jnp.int32, shape, 0)
    member_ids = lax.broadcasted_iota(jnp.int32, shape, 1)
    forced_zero = (block_ids == 0) & (slot_ids == 0)
    forced_last = (leaf_ids == 0) & (member_ids == 0) & (block_ids == blocks - 1) & (slot_ids == slots - 1)
    scores = jnp.where(forced_zero | forced_last, -1, scores)
    ranked = scores * 64 + slot_ids
    order = jnp.argsort(ranked, axis=3)[:, :, :, :count].astype(jnp.int32)
    shifted = jnp.concatenate([order[:, :, :, :1], order[:, :, :, :count - 1]], axis=3)
    reversed_order = jnp.flip(order, axis=3)
    first_block = lax.broadcasted_iota(jnp.int32, (LEAVES, FRONTS_PER_LEVEL, blocks, count), 2) == 0
    assigned = jnp.where(first_block, shifted, reversed_order)
    block_base = lax.broadcasted_iota(jnp.int32, (LEAVES, FRONTS_PER_LEVEL, blocks, count), 2) * slots
    full = (block_base + assigned).reshape(LEAVES, FRONTS_PER_LEVEL, blocks * count // 4, 4)
    kept_block = full[:, :, :, 1:]
    return kept_block.reshape(LEAVES, FRONTS_PER_LEVEL, 3 * (blocks * count // 4)).astype(jnp.int32)


def shard_levels(rng, dims, pieces, least, high):
    def one(position, shards_of):
        steps = jax.random.uniform(jax.random.fold_in(jax.random.fold_in(rng, 6), position), (shards_of,), jnp.float32, least / len(pieces), high / len(pieces))
        return jnp.repeat(jnp.exp(steps), dims[position] // shards_of).reshape((-1,) + (1,) * (len(dims) - position - 1))

    gain = one(*pieces[0])
    for cut in pieces[1:]:
        gain = gain * one(*cut)
    return gain


def setup_inputs(seed: int = 0) -> dict:
    splits = jax.random.split(jax.random.key(seed), 4)
    leaf_fronts = draw_leaf_fronts(jax.random.fold_in(splits[3], 71), 0)
    screen_weights = jnp.clip(jnp.exp(math.log(2.0) - 2.9957323 * jax.random.uniform(splits[1], (LEAVES, FRONTS_PER_LEVEL, M2 // 2), jnp.float32) ** shard_levels(splits[1], (LEAVES, FRONTS_PER_LEVEL, M2 // 2), ((0, 32), (2, 8)), -0.2, 0.2)), 0.1, 2.0)
    parent_tile_index = draw_parent_tile_index(jax.random.fold_in(splits[3], 71), 0)
    return dict(leaf_fronts=leaf_fronts, screen_weights=screen_weights, parent_tile_index=parent_tile_index)


def invert_block(corner_block):
    factor = jnp.linalg.cholesky(corner_block)
    identity = jnp.eye(corner_block.shape[-1], dtype=jnp.float32)
    return jax.scipy.linalg.solve_triangular(factor, identity, lower=True)

def factor_leaf(front_matrix):
    column_block = front_matrix.reshape(FRONT_ORDER_M1, ELIMINATED_TILES, 4, PANEL_WIDTH)[:, :, 0, :].reshape(FRONT_ORDER_M1, SEPARATOR_ONE)
    corner_block = column_block.reshape(ELIMINATED_TILES, 4, PANEL_WIDTH, SEPARATOR_ONE)[:, 0].reshape(SEPARATOR_ONE, SEPARATOR_ONE)
    inverse = invert_block(corner_block)
    return jnp.dot(column_block, inverse.T, precision=lax.Precision.HIGHEST)

def factor_parent(parent):
    inverse = invert_block(parent[:PANEL_WIDTH, :PANEL_WIDTH])
    return jnp.dot(parent[:, :PANEL_WIDTH], inverse.T, precision=lax.Precision.HIGHEST)

def parent_base(weights_natural):
    row_ids = lax.broadcasted_iota(jnp.int32, (M2, M2), 0)
    col_ids = lax.broadcasted_iota(jnp.int32, (M2, M2), 1)
    inside = row_ids < SEP2
    diagonal = jnp.where(row_ids == col_ids, weights_natural[:, None] + jnp.where(inside, 4.0, 0.0), 0.0)
    neighbour = jnp.where(inside & (col_ids < SEP2) & (jnp.abs(row_ids - col_ids) == 1), 1.0, 0.0)
    return diagonal - neighbour

def contribution(schur_update):
    kept_block = 3 * SEPARATOR_ONE
    row_block = schur_update.reshape(ELIMINATED_TILES, 4, PANEL_WIDTH, FRONT_ORDER_M1)[:, 1:].reshape(kept_block, FRONT_ORDER_M1)
    return row_block.reshape(kept_block, ELIMINATED_TILES, 4, PANEL_WIDTH)[:, :, 1:].reshape(kept_block, kept_block)

def add_child(parent, schur_update, child_map):
    tile_blocks = 3 * ELIMINATED_TILES
    count = M2 // PANEL_WIDTH
    inner = contribution(schur_update).reshape(tile_blocks, PANEL_WIDTH, tile_blocks, PANEL_WIDTH).transpose(0, 2, 1, 3)
    grid = parent.reshape(count, PANEL_WIDTH, count, PANEL_WIDTH).transpose(0, 2, 1, 3)
    grid = grid.at[child_map[:, None], child_map[None, :]].add(inner)
    return grid.transpose(0, 2, 1, 3).reshape(M2, M2)

def device_rows(matrix):
    width = matrix.shape[1]
    split = matrix.reshape(N_FRONT, 2, ROWS2, width).transpose(1, 0, 2, 3)
    return split.reshape(2, N_FRONT * ROWS2, width)

def one_pair(inputs):
    pair_fronts, pair_weights, pair_maps = inputs
    leaf_list, panel_list, update_list = ([], [], [])
    for member in range(FRONTS_PER_LEVEL):
        panels = []
        schurs = []
        for child in range(2):
            front_matrix = pair_fronts[child, member]
            panel = factor_leaf(front_matrix)
            panels.append(panel)
            schurs.append(front_matrix - jnp.dot(panel, panel.T, precision=lax.Precision.HIGHEST))
        natural = pair_weights[:, member].reshape(2, N_FRONT, ROWS2).transpose(1, 0, 2).reshape(M2)
        parent = parent_base(natural)
        parent = add_child(parent, schurs[0], pair_maps[0, member])
        parent = add_child(parent, schurs[1], pair_maps[1, member])
        panel_two = factor_parent(parent)
        update = parent[:, PANEL_WIDTH:] - jnp.dot(panel_two, panel_two[PANEL_WIDTH:, :].T, precision=lax.Precision.HIGHEST)
        leaf_list.append(jnp.stack(panels))
        panel_list.append(device_rows(panel_two))
        update_list.append(device_rows(update))
    return (jnp.stack(leaf_list, 1), jnp.stack(panel_list, 1), jnp.stack(update_list, 1))

def reference(leaf_fronts, screen_weights, parent_tile_index):
    front_pairs = LEAVES // 2
    fronts_paired = leaf_fronts.reshape(front_pairs, 2, FRONTS_PER_LEVEL, FRONT_ORDER_M1, FRONT_ORDER_M1)
    weights_paired = screen_weights.reshape(front_pairs, 2, FRONTS_PER_LEVEL, M2 // 2)
    paired_tile_maps = parent_tile_index.reshape(front_pairs, 2, FRONTS_PER_LEVEL, FRONT_TILES_ONE - ELIMINATED_TILES)
    leaf_all, panel_all, update_all = lax.map(one_pair, (fronts_paired, weights_paired, paired_tile_maps))
    leaf_panel = leaf_all.reshape(LEAVES, FRONTS_PER_LEVEL, FRONT_ORDER_M1, SEPARATOR_ONE)
    parent_panel = panel_all.reshape(LEAVES, FRONTS_PER_LEVEL, M2 // 2, PANEL_WIDTH)
    parent_update = update_all.reshape(LEAVES, FRONTS_PER_LEVEL, M2 // 2, M2 - PANEL_WIDTH)
    return (leaf_panel, parent_panel, parent_update)
```

```python
import functools

import jax
import jax.numpy as jnp
from jax import lax
from jax.experimental import pallas as pl
from jax.experimental.pallas import tpu as pltpu
from jax.sharding import PartitionSpec as P

MESH = pl.DeviceIdType.MESH
HIGHEST = lax.Precision.HIGHEST
NT = (((1,), (1,)), ((), ()))
NN = (((1,), (0,)), ((), ()))
TN = (((0,), (0,)), ((), ()))
TILE = 128
SEP2_TILES = 8
f32 = jnp.float32
bf16 = jnp.bfloat16


def exact_dot(a, b, dims):
    return lax.dot_general(a, b, dims, precision=HIGHEST, preferred_element_type=f32)


def thirds(x):
    high = x.astype(bf16)
    rest = x - high.astype(f32)
    mid = rest.astype(bf16)
    low = (rest - mid.astype(f32)).astype(bf16)
    return high, mid, low


def halves(x):
    high = x.astype(bf16)
    return high, (x - high.astype(f32)).astype(bf16)


def left_stack(high, low):
    return jnp.concatenate([high, low, high], axis=1)


def right_stack(high, low):
    return jnp.concatenate([high, high, low], axis=1)


def stack_dot(left, right):
    return lax.dot_general(left, right, NT, preferred_element_type=f32)


def start_block(block, mat, tile, upper):
    row = lax.broadcasted_iota(jnp.int32, (TILE, TILE), 0)
    col = lax.broadcasted_iota(jnp.int32, (TILE, TILE), 1)
    mat[:, :TILE] = block
    mat[:, TILE:] = (row == col).astype(f32)
    tile[...] = mat[0:8, :]
    upper[...] = jnp.zeros_like(upper)


def twice(x):
    return jnp.concatenate([x, x], axis=1)


def factor_panel(step, mat, tile, upper, inv):
    base = step * 8
    sub = lax.broadcasted_iota(jnp.int32, (8, TILE), 0)
    sub_wide = lax.broadcasted_iota(jnp.int32, (8, 2 * TILE), 0)
    high, mid, low = thirds(upper[...])
    left = jnp.concatenate([high, high, mid, high, low, mid], axis=0)[:, :TILE]
    right = jnp.concatenate([high, mid, high, low, high, mid], axis=0)
    mat[...] -= lax.dot_general(left, right, TN, preferred_element_type=f32)
    rows = tile[...]
    entry = {}
    for j in range(8):
        picked = jnp.take_along_axis(rows[:, :TILE], jnp.full((8, TILE), base + j, jnp.int32), axis=1)
        for i in range(j, 8):
            entry[i, j] = jnp.broadcast_to(picked[i : i + 1, :], (8, TILE))
    done = []
    packed = jnp.zeros((8, 2 * TILE), f32)
    for j in range(8):
        pivot = entry[j, j]
        scale = lax.rsqrt(pivot)
        scale = scale * (1.5 - 0.5 * pivot * scale * scale)
        for i in range(j + 1, 8):
            entry[i, j] = entry[i, j] * scale
        for i in range(j + 1, 8):
            for k in range(j + 1, i + 1):
                entry[i, k] = entry[i, k] - entry[i, j] * entry[k, j]
        row = jnp.broadcast_to(rows[j : j + 1, :], (8, 2 * TILE))
        for p in range(j):
            row = row - twice(entry[j, p]) * done[p]
        row = row * twice(scale)
        done.append(row)
        packed = jnp.where(sub_wide == j, row, packed)
    upper[...] = packed
    inv[pl.ds(pl.multiple_of(base, 8), 8), :] = packed[:, TILE:]
    after = pl.multiple_of(jnp.minimum(base + 8, TILE - 8), 8)
    total = mat[pl.ds(after, 8), :]
    for p in range(8):
        weight = jnp.take_along_axis(done[p][:, :TILE], after + sub, axis=1)
        total = total - twice(weight) * done[p]
    tile[...] = total


def exchange_kernel(front, weights, gathered, sibling_rows, weight_rows, local_sem, send_sem, recv_sem, row_send, row_recv):
    leaf = lax.axis_index("leaf")
    front_id = lax.axis_index("front")
    half = lax.rem(leaf, 2)
    chip = lax.div(front_id, 2)
    core = lax.rem(front_id, 2)
    chips = lax.div(lax.axis_size("front"), 2)

    def chip_at(offset):
        return lax.rem(chip + offset + chips, chips)

    sibling = (leaf + 1 - 2 * half, front_id)
    right = (leaf, chip_at(1) * 2 + core)
    left = (leaf, chip_at(-1) * 2 + core)
    partner = (leaf, front_id + 1 - 2 * core)
    everyone = (sibling, right, left, partner)

    weight_rows[0:1, :] = weights[0:1, 0:TILE]
    weight_rows[1:2, :] = weights[0:1, TILE : 2 * TILE]
    weight_rows[2:8, :] = jnp.zeros((6, TILE), f32)
    staged = []

    def stage(src, dst):
        copy = pltpu.make_async_copy(src, dst, local_sem.at[len(staged)])
        copy.start()
        staged.append(copy)

    for r in range(2):
        slot = gathered.at[half, 2 * front_id + r]
        rows = pl.ds(r * TILE, TILE)
        for k in range(4):
            stage(front.at[rows, pl.ds(4 * k * TILE, TILE)], slot.at[:, pl.ds(k * TILE, TILE)])
        stage(front.at[pl.ds(r * TILE + 8, TILE - 8), pl.ds(TILE, TILE)], slot.at[pl.ds(8, TILE - 8), pl.ds(4 * TILE, TILE)])
        head = slot.at[pl.ds(0, 8), pl.ds(4 * TILE, TILE)]
        if r == 1:
            stage(front.at[pl.ds(TILE, 8), pl.ds(TILE, TILE)], head)
        else:
            number = len(staged)

            @pl.when(core == 1)
            def _():
                pltpu.make_async_copy(front.at[pl.ds(0, 8), pl.ds(TILE, TILE)], head, local_sem.at[number]).start()

            @pl.when(core == 0)
            def _():
                pltpu.make_async_copy(weight_rows, head, local_sem.at[number]).start()

            staged.append(pltpu.make_async_copy(weight_rows, head, local_sem.at[number]))

    barrier = pltpu.get_barrier_semaphore()
    for device in everyone:
        pl.semaphore_signal(barrier, inc=1, device_id=device, device_id_type=MESH)
    pl.semaphore_wait(barrier, 4)
    for copy in staged:
        copy.wait()

    sends = []

    def slot_of(child, offset, r, other=False):
        c = 1 - core if other else core
        return child, chip_at(offset) * 4 + c * 2 + r

    def send(where, device):
        child, t = where
        copy = pltpu.make_async_remote_copy(
            src_ref=gathered.at[child, t],
            dst_ref=gathered.at[child, t],
            send_sem=send_sem.at[len(sends)],
            recv_sem=recv_sem.at[child, t],
            device_id=device,
            device_id_type=MESH,
        )
        copy.start()
        sends.append(copy)

    def arrive(where):
        child, t = where
        pltpu.make_async_remote_copy(
            src_ref=gathered.at[child, t],
            dst_ref=gathered.at[child, t],
            send_sem=send_sem.at[0],
            recv_sem=recv_sem.at[child, t],
            device_id=partner,
            device_id_type=MESH,
        ).wait_recv()

    own, other = half, 1 - half
    for r in range(2):
        for device in everyone:
            send(slot_of(own, 0, r), device)

    def row_copy(r, g):
        return pltpu.make_async_remote_copy(
            src_ref=front.at[pl.ds(r * TILE, TILE), pl.ds((4 * g + 1) * TILE, 3 * TILE)],
            dst_ref=sibling_rows.at[pl.ds(r * TILE, TILE), pl.ds(3 * g * TILE, 3 * TILE)],
            send_sem=row_send.at[r, g],
            recv_sem=row_recv.at[r, g],
            device_id=sibling,
            device_id_type=MESH,
        )

    def forward(child, offset, r, *devices):
        where = slot_of(child, offset, r)
        arrive(where)
        for device in devices:
            send(where, device)

    forward(own, -1, 0, right, partner)
    forward(own, 1, 0, partner)
    forward(other, 0, 0, right, left, partner)
    forward(other, 0, 1, right, left, partner)
    for g in range(4):
        row_copy(1, g).start()

    @pl.when(core == 1)
    def _():
        for g in range(4):
            row_copy(0, g).start()

    forward(own, 1, 1, left, partner)
    forward(own, -1, 1, partner)
    forward(other, -1, 0, right, partner)
    forward(other, 1, 0, partner)
    forward(other, 1, 1, left, partner)
    forward(other, -1, 1, partner)
    forward(own, 2, 0, partner)
    forward(own, 2, 1, partner)
    forward(other, 2, 0, partner)
    forward(other, 2, 1, partner)
    for child in (own, other):
        for offset in (0, -1, 1, 2):
            for r in range(2):
                arrive(slot_of(child, offset, r, True))
    for copy in sends:
        copy.wait_send()
    for g in range(4):
        row_copy(1, g).wait()

    @pl.when(core == 1)
    def _():
        for g in range(4):
            row_copy(0, g).wait()


def exchange(front, weights):
    rows, width = front.shape
    tiles = width // TILE
    return pl.pallas_call(
        exchange_kernel,
        out_shape=(
            jax.ShapeDtypeStruct((2, tiles, TILE, 5 * TILE), f32),
            jax.ShapeDtypeStruct((rows, 12 * TILE), f32),
        ),
        in_specs=[pl.BlockSpec(memory_space=pl.ANY), pl.BlockSpec(memory_space=pltpu.VMEM)],
        out_specs=(pl.BlockSpec(memory_space=pl.ANY), pl.BlockSpec(memory_space=pl.ANY)),
        scratch_shapes=[
            pltpu.VMEM((8, TILE), f32),
            pltpu.SemaphoreType.DMA((12,)),
            pltpu.SemaphoreType.DMA((30,)),
            pltpu.SemaphoreType.DMA((2, tiles)),
            pltpu.SemaphoreType.DMA((2, 4)),
            pltpu.SemaphoreType.DMA((2, 4)),
        ],
        compiler_params=pltpu.CompilerParams(collective_id=0, has_side_effects=True),
        name="exchange",
    )(front, weights)


def corner_kernel(gathered, factors, corner, inv, mat, tile, upper, sem):
    copies = []
    for child in range(2):
        for k in range(4):
            copy = pltpu.make_async_copy(
                gathered.at[child, 4 * k, :, pl.ds(0, 4 * TILE)],
                corner.at[child, pl.ds(k * TILE, TILE), :],
                sem.at[child, k],
            )
            copy.start()
            copies.append(copy)
    for copy in copies:
        copy.wait()
    for k in range(4):
        here = slice(k * TILE, (k + 1) * TILE)
        for child in range(2):
            start_block(corner[child, here, here], mat.at[child], tile.at[child], upper.at[child])

        @pl.loop(0, TILE // 8)
        def _(step):
            for child in range(2):
                factor_panel(step, mat.at[child], tile.at[child], upper.at[child], inv.at[child])

        for child in range(2):
            finish_block(k, corner.at[child], inv.at[child], factors.at[child])


def finish_block(k, corner, inv, factors):
    here = slice(k * TILE, (k + 1) * TILE)
    inverse = inv[...]
    level, place = divmod(k, 2)
    if place == 0:
        factors[level, 0:TILE, 0:TILE] = inverse
        factors[level, 0:TILE, TILE:] = jnp.zeros((TILE, TILE), f32)
    else:
        before = slice((k - 1) * TILE, k * TILE)
        middle = exact_dot(corner[here, before], factors[level, 0:TILE, 0:TILE], NN)
        factors[level, TILE:, 0:TILE] = -exact_dot(inverse, middle, NN)
        factors[level, TILE:, TILE:] = inverse
    if k < 3:
        rest = slice((k + 1) * TILE, 4 * TILE)
        below = exact_dot(corner[rest, here], inverse, NT)
        corner[rest, here] = below
        corner[rest, rest] -= exact_dot(below, below, NT)
        if level == 0:
            cut = (1 - place) * TILE
            factors[2, :, place * TILE : (place + 1) * TILE] = below[cut:, :]


def factor_corners(gathered):
    return pl.pallas_call(
        corner_kernel,
        out_shape=jax.ShapeDtypeStruct((2, 3, 2 * TILE, 2 * TILE), f32),
        in_specs=[pl.BlockSpec(memory_space=pl.ANY)],
        out_specs=pl.BlockSpec(memory_space=pltpu.VMEM),
        scratch_shapes=[
            pltpu.VMEM((2, 4 * TILE, 4 * TILE), f32),
            pltpu.VMEM((2, TILE, TILE), f32),
            pltpu.VMEM((2, TILE, 2 * TILE), f32),
            pltpu.VMEM((2, 8, 2 * TILE), f32),
            pltpu.VMEM((2, 8, 2 * TILE), f32),
            pltpu.SemaphoreType.DMA((2, 4)),
        ],
        compiler_params=pltpu.CompilerParams(vmem_limit_bytes=40 * 2**20),
        name="corners",
    )(gathered)


def assemble_kernel(
    index, gathered, front, sibling_rows, factors, weights,
    leaf_panel, parent_panel, parent_update,
    chunk, own_front, sib_front, weight_rows, solver, high, low, column, parent, parent_high, parent_low,
    inv, mat, tile, upper, child_of, sem, row_sem,
):
    leaf = lax.axis_index("leaf")
    front_id = lax.axis_index("front")
    half = lax.rem(leaf, 2)
    first = leaf - half

    loads = {}
    for g in range(4):
        for child in range(2):
            loads[child, g] = pltpu.make_async_copy(
                gathered.at[child, pl.ds(4 * g + 1, 3)], chunk.at[child, g], sem.at[child, g]
            )
            loads[child, g].start()
    row_loads = [
        pltpu.make_async_copy(front, own_front, row_sem.at[0]),
        pltpu.make_async_copy(sibling_rows, sib_front, row_sem.at[1]),
        pltpu.make_async_copy(gathered.at[0, 0, pl.ds(0, 8), pl.ds(4 * TILE, TILE)], weight_rows, row_sem.at[2]),
    ]
    for copy in row_loads:
        copy.start()

    @pl.loop(0, 32)
    def _(p):
        child_of[0, p] = -1
        child_of[1, p] = -1

    for child in range(2):
        for a in range(12):
            child_of[child, index[first + child, a]] = a

    for child in range(2):
        for j in range(3):
            solver[child, j] = right_stack(*halves(factors[child, j]))

    def solve(child, columns):
        one = stack_dot(left_stack(*halves(columns[:, : 2 * TILE])), solver[child, 0])
        one_high, one_low = halves(one)
        two = columns[:, 2 * TILE :] - stack_dot(left_stack(one_high, one_low), solver[child, 2])
        two = stack_dot(left_stack(*halves(two)), solver[child, 1])
        return one, two

    for g in range(4):
        for child in range(2):
            loads[child, g].wait()
            block = chunk[child, g].reshape(3 * TILE, 5 * TILE)
            one, two = solve(child, block[:, : 4 * TILE])
            whole_high, whole_low = halves(jnp.concatenate([one, two], axis=1))
            high[child, pl.ds(3 * g, 3)] = whole_high.reshape(3, TILE, 4 * TILE)
            low[child, pl.ds(3 * g, 3)] = whole_low.reshape(3, TILE, 4 * TILE)
            product = stack_dot(left_stack(whole_high, whole_low), right_stack(high[child, 0], low[child, 0]))
            column[child, pl.ds(3 * g, 3)] = (block[:, 4 * TILE :] - product).reshape(3, TILE, TILE)

    for copy in row_loads:
        copy.wait()
    own_columns = jnp.concatenate([own_front[:, 4 * k * TILE : (4 * k + 1) * TILE] for k in range(4)], axis=1)
    one, two = solve(half, own_columns)
    leaf_panel[:, : 2 * TILE] = one
    leaf_panel[:, 2 * TILE :] = two

    row = lax.broadcasted_iota(jnp.int32, (TILE, TILE), 0)
    col = lax.broadcasted_iota(jnp.int32, (TILE, TILE), 1)
    near = jnp.where(jnp.abs(row - col) == 1, 1.0, 0.0)
    above = jnp.where((row == 0) & (col == TILE - 1), 1.0, 0.0)
    under = jnp.where((row == TILE - 1) & (col == 0), 1.0, 0.0)

    @pl.loop(0, 32)
    def _(p):
        total = jnp.zeros((TILE, TILE), f32)
        for child in range(2):
            a = child_of[child, p]
            total = total + jnp.where(a >= 0, column[child, jnp.maximum(a, 0)], 0.0)
        parent[p] = total

    parent[0] += jnp.where(row == col, weight_rows[0:1, :] + 4.0, 0.0) - near
    parent[1] -= above

    start_block(parent[0], mat, tile, upper)

    @pl.loop(0, TILE // 8)
    def _(step):
        factor_panel(step, mat, tile, upper, inv)

    last = right_stack(*halves(inv[...]))
    for q in range(8):
        block = parent[4 * q : 4 * q + 4].reshape(4 * TILE, TILE)
        done = stack_dot(left_stack(*halves(block)), last)
        parent[4 * q : 4 * q + 4] = done.reshape(4, TILE, TILE)
        done_high, done_low = halves(done)
        parent_high[4 * q * TILE : 4 * (q + 1) * TILE, :] = done_high
        parent_low[4 * q * TILE : 4 * (q + 1) * TILE, :] = done_low

    place = 4 * front_id + 2 * half
    parent_panel[...] = parent[pl.ds(place, 2)].reshape(2 * TILE, TILE)
    here = pl.ds(pl.multiple_of(place * TILE, TILE), 2 * TILE)
    mine = left_stack(parent_high[here, :], parent_low[here, :])
    for start in range(TILE, 32 * TILE, 4 * TILE):
        stop = min(start + 4 * TILE, 32 * TILE)
        there = right_stack(parent_high[start:stop, :], parent_low[start:stop, :])
        parent_update[:, start - TILE : stop - TILE] = -stack_dot(mine, there)

    def columns_of(p):
        return pl.ds(pl.multiple_of((p - 1) * TILE, TILE), TILE)

    for kin in range(2):
        child = half if kin == 0 else 1 - half
        source = own_front if kin == 0 else sib_front
        for r in range(2):
            a = child_of[child, place + r]
            rows = pl.ds(r * TILE, TILE)

            @pl.when(a >= 0)
            def _():
                local = 4 * lax.div(a, 3) + lax.rem(a, 3) + 1 - 2 * front_id
                source_rows = pl.ds(pl.multiple_of(local * TILE, TILE), TILE)
                lead = left_stack(high[child, a], low[child, a])
                for g in range(4):
                    others = right_stack(
                        high[child, pl.ds(3 * g, 3)].reshape(3 * TILE, 4 * TILE),
                        low[child, pl.ds(3 * g, 3)].reshape(3 * TILE, 4 * TILE),
                    )
                    product = stack_dot(lead, others)
                    for m in range(3):
                        b = 3 * g + m
                        p = index[first + child, b]
                        t = 4 * g + m + 1 if kin == 0 else b
                        value = source[source_rows, t * TILE : (t + 1) * TILE] - product[:, m * TILE : (m + 1) * TILE]
                        if b == 0:
                            continue
                        parent_update[rows, columns_of(p)] += value

    for r in range(2):
        p = place + r
        rows = slice(r * TILE, (r + 1) * TILE)
        own_weights = weights[0:1, r * TILE : (r + 1) * TILE]
        inside = p < SEP2_TILES

        @pl.when(p >= 1)
        def _():
            extra = jnp.where(inside, 1.0, 0.0)
            parent_update[rows, columns_of(p)] += jnp.where(row == col, own_weights + 4.0 * extra, 0.0) - near * extra

        @pl.when((p >= 2) & inside)
        def _():
            parent_update[rows, columns_of(p - 1)] -= above

        @pl.when(p + 1 < SEP2_TILES)
        def _():
            parent_update[rows, columns_of(p + 1)] -= under


def assemble(index, gathered, front, sibling_rows, factors, weights):
    rows, width = front.shape
    anywhere = pl.BlockSpec(memory_space=pl.ANY)
    local = pl.BlockSpec(memory_space=pltpu.VMEM)
    return pl.pallas_call(
        assemble_kernel,
        out_shape=(
            jax.ShapeDtypeStruct((rows, 4 * TILE), f32),
            jax.ShapeDtypeStruct((rows, TILE), f32),
            jax.ShapeDtypeStruct((rows, 31 * TILE), f32),
        ),
        in_specs=[pl.BlockSpec(memory_space=pltpu.SMEM), anywhere, anywhere, anywhere, local, local],
        out_specs=(local, local, local),
        scratch_shapes=[
            pltpu.VMEM((2, 4, 3, TILE, 5 * TILE), f32),
            pltpu.VMEM((rows, width), f32),
            pltpu.VMEM((rows, 12 * TILE), f32),
            pltpu.VMEM((8, TILE), f32),
            pltpu.VMEM((2, 3, 2 * TILE, 6 * TILE), bf16),
            pltpu.VMEM((2, 12, TILE, 4 * TILE), bf16),
            pltpu.VMEM((2, 12, TILE, 4 * TILE), bf16),
            pltpu.VMEM((2, 12, TILE, TILE), f32),
            pltpu.VMEM((32, TILE, TILE), f32),
            pltpu.VMEM((32 * TILE, TILE), bf16),
            pltpu.VMEM((32 * TILE, TILE), bf16),
            pltpu.VMEM((TILE, TILE), f32),
            pltpu.VMEM((TILE, 2 * TILE), f32),
            pltpu.VMEM((8, 2 * TILE), f32),
            pltpu.VMEM((8, 2 * TILE), f32),
            pltpu.SMEM((2, 32), jnp.int32),
            pltpu.SemaphoreType.DMA((2, 4)),
            pltpu.SemaphoreType.DMA((3,)),
        ],
        compiler_params=pltpu.CompilerParams(vmem_limit_bytes=56 * 2**20),
        name="assemble",
    )(index, gathered, front, sibling_rows, factors, weights)


def on_device(leaf_fronts, screen_weights, parent_tile_index):
    front = leaf_fronts[0, 0]
    weights = screen_weights[0]
    index = parent_tile_index[:, 0]
    gathered, sibling_rows = exchange(front, weights)
    factors = factor_corners(gathered)
    leaf_panel, parent_panel, parent_update = assemble(index, gathered, front, sibling_rows, factors, weights)
    return leaf_panel[None, None], parent_panel[None, None], parent_update[None, None]


def solution(mesh):
    rows = P("leaf", None, "front", None)
    return jax.shard_map(
        on_device,
        mesh=mesh,
        in_specs=(rows, P("leaf", None, "front"), P()),
        out_specs=(rows, rows, rows),
        check_vma=False,
    )
```

```python
import functools

import jax
import jax.numpy as jnp
from jax import lax
from jax.experimental import pallas as pl
from jax.experimental.pallas import tpu as pltpu
from jax.sharding import PartitionSpec as P

MESH = pl.DeviceIdType.MESH
HIGHEST = lax.Precision.HIGHEST
NT = (((1,), (1,)), ((), ()))
NN = (((1,), (0,)), ((), ()))
TN = (((0,), (0,)), ((), ()))
TILE = 128
SEP2_TILES = 8
f32 = jnp.float32
bf16 = jnp.bfloat16


def exact_dot(a, b, dims):
    return lax.dot_general(a, b, dims, precision=HIGHEST, preferred_element_type=f32)


def thirds(x):
    high = x.astype(bf16)
    rest = x - high.astype(f32)
    mid = rest.astype(bf16)
    low = (rest - mid.astype(f32)).astype(bf16)
    return high, mid, low


def halves(x):
    high = x.astype(bf16)
    return high, (x - high.astype(f32)).astype(bf16)


def left_stack(high, low):
    return jnp.concatenate([high, low, high], axis=1)


def right_stack(high, low):
    return jnp.concatenate([high, high, low], axis=1)


def stack_dot(left, right):
    return lax.dot_general(left, right, NT, preferred_element_type=f32)


def start_block(block, mat, tile, upper):
    row = lax.broadcasted_iota(jnp.int32, (TILE, TILE), 0)
    col = lax.broadcasted_iota(jnp.int32, (TILE, TILE), 1)
    mat[:, :TILE] = block
    mat[:, TILE:] = (row == col).astype(f32)
    tile[...] = mat[0:8, :]
    upper[...] = jnp.zeros_like(upper)


def twice(x):
    return jnp.concatenate([x, x], axis=1)


def factor_panel(step, mat, tile, upper, inv):
    base = step * 8
    sub = lax.broadcasted_iota(jnp.int32, (8, TILE), 0)
    sub_wide = lax.broadcasted_iota(jnp.int32, (8, 2 * TILE), 0)
    high, mid, low = thirds(upper[...])
    left = jnp.concatenate([high, high, mid, high, low, mid], axis=0)[:, :TILE]
    right = jnp.concatenate([high, mid, high, low, high, mid], axis=0)
    mat[...] -= lax.dot_general(left, right, TN, preferred_element_type=f32)
    rows = tile[...]
    entry = {}
    for j in range(8):
        picked = jnp.take_along_axis(rows[:, :TILE], jnp.full((8, TILE), base + j, jnp.int32), axis=1)
        for i in range(j, 8):
            entry[i, j] = jnp.broadcast_to(picked[i : i + 1, :], (8, TILE))
    done = []
    packed = jnp.zeros((8, 2 * TILE), f32)
    for j in range(8):
        pivot = entry[j, j]
        scale = lax.rsqrt(pivot)
        scale = scale * (1.5 - 0.5 * pivot * scale * scale)
        for i in range(j + 1, 8):
            entry[i, j] = entry[i, j] * scale
        for i in range(j + 1, 8):
            for k in range(j + 1, i + 1):
                entry[i, k] = entry[i, k] - entry[i, j] * entry[k, j]
        row = jnp.broadcast_to(rows[j : j + 1, :], (8, 2 * TILE))
        for p in range(j):
            row = row - twice(entry[j, p]) * done[p]
        row = row * twice(scale)
        done.append(row)
        packed = jnp.where(sub_wide == j, row, packed)
    upper[...] = packed
    inv[pl.ds(pl.multiple_of(base, 8), 8), :] = packed[:, TILE:]
    after = pl.multiple_of(jnp.minimum(base + 8, TILE - 8), 8)
    total = mat[pl.ds(after, 8), :]
    for p in range(8):
        weight = jnp.take_along_axis(done[p][:, :TILE], after + sub, axis=1)
        total = total - twice(weight) * done[p]
    tile[...] = total


def gather_factor_kernel(
    front, weights,
    sibling_rows, high, low, column, top, top_inv, own_panel,
    gathered, corner_in, corner, own_rows, factors, solver, lead, inv, mat, tile, upper,
    local_sem, first_send, first_recv, bulk_send, bulk_recv, row_send, row_recv,
):
    leaf = lax.axis_index("leaf")
    front_id = lax.axis_index("front")
    half = lax.rem(leaf, 2)
    chip = lax.div(front_id, 2)
    core = lax.rem(front_id, 2)
    chips = lax.div(lax.axis_size("front"), 2)
    own, other = half, 1 - half

    def chip_at(offset):
        return lax.rem(chip + offset + chips, chips)

    sibling = (leaf + 1 - 2 * half, front_id)
    right = (leaf, chip_at(1) * 2 + core)
    left = (leaf, chip_at(-1) * 2 + core)
    partner = (leaf, front_id + 1 - 2 * core)

    staged = []

    def stage(src, dst, condition=None):
        copy = pltpu.make_async_copy(src, dst, local_sem.at[len(staged)])
        staged.append((condition, copy))
        when(condition, copy.start)

    def when(condition, action):
        if condition is None:
            action()
        else:
            pl.when(condition)(lambda: action())

    def stage_row(r, slot, condition=None):
        rows = pl.ds(r * TILE, TILE)
        for k in range(4):
            stage(front.at[rows, pl.ds(4 * k * TILE, TILE)], slot.at[:, pl.ds(k * TILE, TILE)], condition)
        stage(front.at[rows, pl.ds(TILE, TILE)], slot.at[:, pl.ds(4 * TILE, TILE)], condition)

    corner_slot = corner_in.at[own, pl.ds(pl.multiple_of(chip * TILE, TILE), TILE)]
    for k in range(4):
        stage(front.at[pl.ds(0, TILE), pl.ds(4 * k * TILE, TILE)], corner_slot.at[:, pl.ds(k * TILE, TILE)], core == 0)
    stage_row(0, gathered.at[own, 3 * chip + 1], core == 1)
    stage_row(1, gathered.at[own, 3 * chip + 2 * core])
    for k in range(4):
        stage(front.at[:, pl.ds(4 * k * TILE, TILE)], own_rows.at[:, pl.ds(k * TILE, TILE)])

    barrier = pltpu.get_barrier_semaphore()
    for device in (sibling, right, left, partner):
        pl.semaphore_signal(barrier, inc=1, device_id=device, device_id_type=MESH)
    pl.semaphore_wait(barrier, 4)
    for condition, copy in staged:
        when(condition, copy.wait)

    @pl.when((core == 0) & (chip == 0) & (half == 0))
    def _():
        corner_in[0, 0:1, TILE : 2 * TILE] = weights[0:1, 0:TILE]

    sends = []

    def remote(ref, send_sem, recv_sem, device):
        return pltpu.make_async_remote_copy(
            src_ref=ref, dst_ref=ref, send_sem=send_sem, recv_sem=recv_sem, device_id=device, device_id_type=MESH
        )

    def first_pieces(child, offset):
        k = chip_at(offset)
        rows = pl.ds(pl.multiple_of(k * TILE, TILE), TILE)
        refs = (
            (None, corner_in.at[child, rows, pl.ds(0, 2 * TILE)]),
            (k >= 2, corner_in.at[child, rows, pl.ds(2 * TILE, 2 * TILE)]),
            (k == 0, gathered.at[child, 0]),
        )
        return [(condition, ref, first_recv.at[child, k, n]) for n, (condition, ref) in enumerate(refs)]

    counts = {"first": 0, "bulk": 0}

    def start(kind, pool, build, device):
        number = counts[kind]
        counts[kind] += 1

        def make():
            condition, ref, recv_sem = build()
            return condition, remote(ref, pool.at[number], recv_sem, device)

        sends.append((kind, make))
        condition, copy = make()
        when(condition, copy.start)

    def first_send_to(child, offset, devices, pieces=(0, 1, 2)):
        for device in devices:
            for n in pieces:
                start("first", first_send, lambda n=n: first_pieces(child, offset)[n], device)

    def first_arrive(child, offset):
        for condition, ref, recv_sem in first_pieces(child, offset):
            when(condition, remote(ref, first_send.at[0], recv_sem, partner).wait_recv)

    def bulk_pieces(child, offset, from_core):
        k = chip_at(offset)
        pieces = []
        for i in range(2):
            a = 3 * k + lax.select(from_core == 1, 1 + i, 0)
            condition = (from_core == 1) if i == 1 else ((from_core == 1) | (k != 0))
            for q in range(2):
                pieces.append((condition, gathered.at[child, a, pl.ds(q * 64, 64)], bulk_recv.at[child, a, q]))
        return pieces

    def bulk_send_to(child, offset, devices, only=None):
        for device in devices:
            for n in range(4):
                if only is None or only == n % 2:
                    start("bulk", bulk_send, lambda n=n: bulk_pieces(child, offset, core)[n], device)

    def bulk_arrive(child, offset, from_core):
        for condition, ref, recv_sem in bulk_pieces(child, offset, from_core):
            when(condition, remote(ref, bulk_send.at[0], recv_sem, partner).wait_recv)

    @pl.when(core == 0)
    def _():
        first_send_to(own, 0, (right, left, sibling, partner))
        first_arrive(own, -1)
        first_send_to(own, -1, (right,), (0, 2))
        first_arrive(own, 1)
        first_send_to(own, 1, (left,), (1,))
        first_arrive(other, 0)
        first_send_to(other, 0, (right, left))
        first_send_to(own, -1, (partner,))
        first_send_to(own, 1, (partner,))
        first_send_to(other, 0, (partner,))
        first_arrive(other, -1)
        first_send_to(other, -1, (right,), (0, 2))
        first_arrive(other, 1)
        first_send_to(other, 1, (left,), (1,))
        first_send_to(other, -1, (partner,))
        first_send_to(other, 1, (partner,))

    bulk_send_to(own, 0, (sibling, right, left, partner))

    @pl.when(core == 0)
    def _():
        for child in (own, other):
            first_arrive(child, 2)
            first_send_to(child, 2, (partner,))

    @pl.when(core == 1)
    def _():
        for child in (own, other):
            for offset in (0, -1, 1, 2):
                first_arrive(child, offset)

    def row_copy(r, g):
        return pltpu.make_async_remote_copy(
            src_ref=front.at[pl.ds(r * TILE, TILE), pl.ds((4 * g + 1) * TILE, 3 * TILE)],
            dst_ref=sibling_rows.at[pl.ds(r * TILE, TILE), pl.ds(3 * g * TILE, 3 * TILE)],
            send_sem=row_send.at[r, g],
            recv_sem=row_recv.at[r, g],
            device_id=sibling,
            device_id_type=MESH,
        )

    def after_block(k):
        if k == 0:
            bulk_arrive(other, 0, core)
            bulk_send_to(other, 0, (right, left, partner))
            for g in range(4):
                row_copy(1, g).start()

            @pl.when(core == 1)
            def _():
                for g in range(4):
                    row_copy(0, g).start()

        if k == 1:
            bulk_arrive(own, -1, core)
            bulk_send_to(own, -1, (right,), 0)
            bulk_send_to(own, -1, (partner,))
            bulk_arrive(own, 1, core)
            bulk_send_to(own, 1, (left,), 1)
            bulk_send_to(own, 1, (partner,))
        if k == 3:
            bulk_arrive(other, -1, core)
            bulk_send_to(other, -1, (right,), 0)
            bulk_send_to(other, -1, (partner,))
            bulk_arrive(other, 1, core)
            bulk_send_to(other, 1, (left,), 1)
            bulk_send_to(other, 1, (partner,))

    corner[...] = corner_in[...]
    for k in range(4):
        here = slice(k * TILE, (k + 1) * TILE)
        for child in range(2):
            start_block(corner[child, here, here], mat.at[child], tile.at[child], upper.at[child])

        @pl.loop(0, TILE // 8)
        def _(step):
            for child in range(2):
                factor_panel(step, mat.at[child], tile.at[child], upper.at[child], inv.at[child])

        for child in range(2):
            finish_block(k, corner.at[child], inv.at[child], factors.at[child])
        after_block(k)

    for child in range(2):
        for j in range(3):
            solver[child, j] = right_stack(*halves(factors[child, j]))

    def solve(child, columns):
        one = stack_dot(left_stack(*halves(columns[:, : 2 * TILE])), solver[child, 0])
        one_high, one_low = halves(one)
        two = columns[:, 2 * TILE :] - stack_dot(left_stack(one_high, one_low), solver[child, 2])
        two = stack_dot(left_stack(*halves(two)), solver[child, 1])
        return one, two

    row = lax.broadcasted_iota(jnp.int32, (TILE, TILE), 0)
    col = lax.broadcasted_iota(jnp.int32, (TILE, TILE), 1)
    near = jnp.where(jnp.abs(row - col) == 1, 1.0, 0.0)
    total = jnp.where(row == col, corner_in[0, 0:1, TILE : 2 * TILE] + 4.0, 0.0) - near
    for child in range(2):
        one_high, one_low = halves(jnp.concatenate(solve(child, gathered[child, 0, :, : 4 * TILE]), axis=1))
        lead[child] = right_stack(one_high, one_low)
        total = total + (gathered[child, 0, :, 4 * TILE :] - stack_dot(left_stack(one_high, one_low), lead[child]))
    top[...] = total
    start_block(total, mat.at[0], tile.at[0], upper.at[0])

    @pl.loop(0, TILE // 8)
    def _(step):
        factor_panel(step, mat.at[0], tile.at[0], upper.at[0], top_inv)

    one, two = solve(own, own_rows[...])
    own_panel[:, : 2 * TILE] = one
    own_panel[:, 2 * TILE :] = two

    def panels(child, offset):
        rows = pl.ds(3 * chip_at(offset), 3)
        block = gathered[child, rows].reshape(3 * TILE, 5 * TILE)
        whole_high, whole_low = halves(jnp.concatenate(solve(child, block[:, : 4 * TILE]), axis=1))
        high[child, rows] = whole_high.reshape(3, TILE, 4 * TILE)
        low[child, rows] = whole_low.reshape(3, TILE, 4 * TILE)
        product = stack_dot(left_stack(whole_high, whole_low), lead[child])
        column[child, rows] = (block[:, 4 * TILE :] - product).reshape(3, TILE, TILE)

    for offset in (0, -1, 1):
        for child in (own, other):
            bulk_arrive(child, offset, 1 - core)
            panels(child, offset)
    for child in (own, other):
        bulk_arrive(child, 2, core)
        bulk_send_to(child, 2, (partner,))
    for child in (own, other):
        bulk_arrive(child, 2, 1 - core)
        panels(child, 2)

    def sent(kind):
        for name, make in sends:
            if name == kind:
                condition, copy = make()
                when(condition, copy.wait_send)

    pl.when(core == 0)(lambda: sent("first"))
    sent("bulk")
    for g in range(4):
        row_copy(1, g).wait()

    @pl.when(core == 1)
    def _():
        for g in range(4):
            row_copy(0, g).wait()


def finish_block(k, corner, inv, factors):
    here = slice(k * TILE, (k + 1) * TILE)
    inverse = inv[...]
    level, place = divmod(k, 2)
    if place == 0:
        factors[level, 0:TILE, 0:TILE] = inverse
        factors[level, 0:TILE, TILE:] = jnp.zeros((TILE, TILE), f32)
    else:
        before = slice((k - 1) * TILE, k * TILE)
        middle = exact_dot(corner[here, before], factors[level, 0:TILE, 0:TILE], NN)
        factors[level, TILE:, 0:TILE] = -exact_dot(inverse, middle, NN)
        factors[level, TILE:, TILE:] = inverse
    if k < 3:
        rest = slice((k + 1) * TILE, 4 * TILE)
        below = exact_dot(corner[rest, here], inverse, NT)
        corner[rest, here] = below
        corner[rest, rest] -= exact_dot(below, below, NT)
        if level == 0:
            cut = (1 - place) * TILE
            factors[2, :, place * TILE : (place + 1) * TILE] = below[cut:, :]


def gather_factor(front, weights):
    rows, width = front.shape
    local = pl.BlockSpec(memory_space=pltpu.VMEM)
    anywhere = pl.BlockSpec(memory_space=pl.ANY)
    return pl.pallas_call(
        gather_factor_kernel,
        out_shape=(
            jax.ShapeDtypeStruct((rows, 12 * TILE), f32),
            jax.ShapeDtypeStruct((2, 12, TILE, 4 * TILE), bf16),
            jax.ShapeDtypeStruct((2, 12, TILE, 4 * TILE), bf16),
            jax.ShapeDtypeStruct((2, 12, TILE, TILE), f32),
            jax.ShapeDtypeStruct((TILE, TILE), f32),
            jax.ShapeDtypeStruct((TILE, TILE), f32),
            jax.ShapeDtypeStruct((rows, 4 * TILE), f32),
        ),
        in_specs=[anywhere, local],
        out_specs=(anywhere, local, local, local, local, local, local),
        scratch_shapes=[
            pltpu.VMEM((2, 12, TILE, 5 * TILE), f32),
            pltpu.VMEM((2, 4 * TILE, 4 * TILE), f32),
            pltpu.VMEM((2, 4 * TILE, 4 * TILE), f32),
            pltpu.VMEM((rows, 4 * TILE), f32),
            pltpu.VMEM((2, 3, 2 * TILE, 2 * TILE), f32),
            pltpu.VMEM((2, 3, 2 * TILE, 6 * TILE), bf16),
            pltpu.VMEM((2, TILE, 12 * TILE), bf16),
            pltpu.VMEM((2, TILE, TILE), f32),
            pltpu.VMEM((2, TILE, 2 * TILE), f32),
            pltpu.VMEM((2, 8, 2 * TILE), f32),
            pltpu.VMEM((2, 8, 2 * TILE), f32),
            pltpu.SemaphoreType.DMA((20,)),
            pltpu.SemaphoreType.DMA((60,)),
            pltpu.SemaphoreType.DMA((2, 4, 3)),
            pltpu.SemaphoreType.DMA((80,)),
            pltpu.SemaphoreType.DMA((2, 12, 2)),
            pltpu.SemaphoreType.DMA((2, 4)),
            pltpu.SemaphoreType.DMA((2, 4)),
        ],
        compiler_params=pltpu.CompilerParams(
            collective_id=0, has_side_effects=True, vmem_limit_bytes=34 * 2**20
        ),
        name="gather_factor",
    )(front, weights)


def assemble_kernel(
    index, front, sibling_rows, weights, high, low, column, top, top_inv, own_panel,
    leaf_panel, parent_panel, parent_update,
    own_front, sib_front, parent, parent_high, parent_low, child_of, row_sem,
):
    leaf = lax.axis_index("leaf")
    front_id = lax.axis_index("front")
    half = lax.rem(leaf, 2)
    first = leaf - half
    row_loads = [
        pltpu.make_async_copy(front, own_front, row_sem.at[0]),
        pltpu.make_async_copy(sibling_rows, sib_front, row_sem.at[1]),
    ]
    for copy in row_loads:
        copy.start()
    leaf_panel[...] = own_panel[...]

    @pl.loop(0, 32)
    def _(p):
        child_of[0, p] = -1
        child_of[1, p] = -1

    for child in range(2):
        for a in range(12):
            child_of[child, index[first + child, a]] = a

    row = lax.broadcasted_iota(jnp.int32, (TILE, TILE), 0)
    col = lax.broadcasted_iota(jnp.int32, (TILE, TILE), 1)
    near = jnp.where(jnp.abs(row - col) == 1, 1.0, 0.0)
    above = jnp.where((row == 0) & (col == TILE - 1), 1.0, 0.0)
    under = jnp.where((row == TILE - 1) & (col == 0), 1.0, 0.0)

    @pl.loop(0, 32)
    def _(p):
        total = jnp.zeros((TILE, TILE), f32)
        for child in range(2):
            a = child_of[child, p]
            total = total + jnp.where(a >= 0, column[child, jnp.maximum(a, 0)], 0.0)
        parent[p] = total

    parent[0] = top[...]
    parent[1] -= above

    last = right_stack(*halves(top_inv[...]))
    for q in range(8):
        block = parent[4 * q : 4 * q + 4].reshape(4 * TILE, TILE)
        done = stack_dot(left_stack(*halves(block)), last)
        parent[4 * q : 4 * q + 4] = done.reshape(4, TILE, TILE)
        done_high, done_low = halves(done)
        parent_high[4 * q * TILE : 4 * (q + 1) * TILE, :] = done_high
        parent_low[4 * q * TILE : 4 * (q + 1) * TILE, :] = done_low

    place = 4 * front_id + 2 * half
    parent_panel[...] = parent[pl.ds(place, 2)].reshape(2 * TILE, TILE)
    here = pl.ds(pl.multiple_of(place * TILE, TILE), 2 * TILE)
    mine = left_stack(parent_high[here, :], parent_low[here, :])
    for start in range(TILE, 32 * TILE, 4 * TILE):
        stop = min(start + 4 * TILE, 32 * TILE)
        there = right_stack(parent_high[start:stop, :], parent_low[start:stop, :])
        parent_update[:, start - TILE : stop - TILE] = -stack_dot(mine, there)

    def columns_of(p):
        return pl.ds(pl.multiple_of((p - 1) * TILE, TILE), TILE)

    for copy in row_loads:
        copy.wait()
    for kin in range(2):
        child = half if kin == 0 else 1 - half
        source = own_front if kin == 0 else sib_front
        for r in range(2):
            a = child_of[child, place + r]
            rows = pl.ds(r * TILE, TILE)

            @pl.when(a >= 0)
            def _():
                local = 4 * lax.div(a, 3) + lax.rem(a, 3) + 1 - 2 * front_id
                source_rows = pl.ds(pl.multiple_of(local * TILE, TILE), TILE)
                lead = left_stack(high[child, a], low[child, a])
                for g in range(4):
                    others = right_stack(
                        high[child, pl.ds(3 * g, 3)].reshape(3 * TILE, 4 * TILE),
                        low[child, pl.ds(3 * g, 3)].reshape(3 * TILE, 4 * TILE),
                    )
                    product = stack_dot(lead, others)
                    for m in range(3):
                        b = 3 * g + m
                        p = index[first + child, b]
                        t = 4 * g + m + 1 if kin == 0 else b
                        value = source[source_rows, t * TILE : (t + 1) * TILE] - product[:, m * TILE : (m + 1) * TILE]
                        if b == 0:
                            continue
                        parent_update[rows, columns_of(p)] += value

    for r in range(2):
        p = place + r
        rows = slice(r * TILE, (r + 1) * TILE)
        own_weights = weights[0:1, r * TILE : (r + 1) * TILE]
        inside = p < SEP2_TILES

        @pl.when(p >= 1)
        def _():
            extra = jnp.where(inside, 1.0, 0.0)
            parent_update[rows, columns_of(p)] += jnp.where(row == col, own_weights + 4.0 * extra, 0.0) - near * extra

        @pl.when((p >= 2) & inside)
        def _():
            parent_update[rows, columns_of(p - 1)] -= above

        @pl.when(p + 1 < SEP2_TILES)
        def _():
            parent_update[rows, columns_of(p + 1)] -= under


def assemble(index, front, weights, sibling_rows, *rest):
    rows, width = front.shape
    anywhere = pl.BlockSpec(memory_space=pl.ANY)
    local = pl.BlockSpec(memory_space=pltpu.VMEM)
    return pl.pallas_call(
        assemble_kernel,
        out_shape=(
            jax.ShapeDtypeStruct((rows, 4 * TILE), f32),
            jax.ShapeDtypeStruct((rows, TILE), f32),
            jax.ShapeDtypeStruct((rows, 31 * TILE), f32),
        ),
        in_specs=[pl.BlockSpec(memory_space=pltpu.SMEM), anywhere, anywhere] + [local] * 7,
        out_specs=(local, local, local),
        scratch_shapes=[
            pltpu.VMEM((rows, width), f32),
            pltpu.VMEM((rows, 12 * TILE), f32),
            pltpu.VMEM((32, TILE, TILE), f32),
            pltpu.VMEM((32 * TILE, TILE), bf16),
            pltpu.VMEM((32 * TILE, TILE), bf16),
            pltpu.SMEM((2, 32), jnp.int32),
            pltpu.SemaphoreType.DMA((2,)),
        ],
        compiler_params=pltpu.CompilerParams(vmem_limit_bytes=30 * 2**20),
        name="assemble",
    )(index, front, sibling_rows, weights, *rest)


def on_device(leaf_fronts, screen_weights, parent_tile_index):
    front = leaf_fronts[0, 0]
    weights = screen_weights[0]
    index = parent_tile_index[:, 0]
    leaf_panel, parent_panel, parent_update = assemble(index, front, weights, *gather_factor(front, weights))
    return leaf_panel[None, None], parent_panel[None, None], parent_update[None, None]


def solution(mesh):
    rows = P("leaf", None, "front", None)
    return jax.shard_map(
        on_device,
        mesh=mesh,
        in_specs=(rows, P("leaf", None, "front"), P()),
        out_specs=(rows, rows, rows),
        check_vma=False,
    )
```

```python
import functools

import jax
import jax.numpy as jnp
from jax import lax
from jax.experimental import pallas as pl
from jax.experimental.pallas import tpu as pltpu
from jax.sharding import PartitionSpec as P

MESH = pl.DeviceIdType.MESH
HIGHEST = lax.Precision.HIGHEST
NT = (((1,), (1,)), ((), ()))
NN = (((1,), (0,)), ((), ()))
TN = (((0,), (0,)), ((), ()))
TILE = 128
SEP2_TILES = 8
f32 = jnp.float32
bf16 = jnp.bfloat16


def exact_dot(a, b, dims):
    return lax.dot_general(a, b, dims, precision=HIGHEST, preferred_element_type=f32)


def thirds(x):
    high = x.astype(bf16)
    rest = x - high.astype(f32)
    mid = rest.astype(bf16)
    low = (rest - mid.astype(f32)).astype(bf16)
    return high, mid, low


def halves(x):
    high = x.astype(bf16)
    return high, (x - high.astype(f32)).astype(bf16)


def left_stack(high, low):
    return jnp.concatenate([high, low, high], axis=1)


def right_stack(high, low):
    return jnp.concatenate([high, high, low], axis=1)


def stack_dot(left, right):
    return lax.dot_general(left, right, NT, preferred_element_type=f32)


def start_block(block, mat, tile, upper):
    row = lax.broadcasted_iota(jnp.int32, (TILE, TILE), 0)
    col = lax.broadcasted_iota(jnp.int32, (TILE, TILE), 1)
    mat[:, :TILE] = block
    mat[:, TILE:] = (row == col).astype(f32)
    tile[...] = mat[0:8, :]
    upper[...] = jnp.zeros_like(upper)


def twice(x):
    return jnp.concatenate([x, x], axis=1)


def factor_panel(step, mat, tile, upper, inv):
    base = step * 8
    sub = lax.broadcasted_iota(jnp.int32, (8, TILE), 0)
    sub_wide = lax.broadcasted_iota(jnp.int32, (8, 2 * TILE), 0)
    high, mid, low = thirds(upper[...])
    left = jnp.concatenate([high, high, mid, high, low, mid], axis=0)[:, :TILE]
    right = jnp.concatenate([high, mid, high, low, high, mid], axis=0)
    mat[...] -= lax.dot_general(left, right, TN, preferred_element_type=f32)
    rows = tile[...]
    cols = [
        jnp.take_along_axis(rows[:, :TILE], jnp.full((8, TILE), base + j, jnp.int32), axis=1) for j in range(8)
    ]
    done = []
    packed = jnp.zeros((8, 2 * TILE), f32)
    entry = {}
    for j in range(8):
        scale = lax.rsqrt(jnp.broadcast_to(cols[j][j : j + 1, :], (8, TILE)))
        column = cols[j] * scale
        for k in range(j + 1, 8):
            entry[k, j] = jnp.broadcast_to(column[k : k + 1, :], (8, TILE))
            cols[k] = cols[k] - column * entry[k, j]
        row = jnp.broadcast_to(rows[j : j + 1, :], (8, 2 * TILE))
        for p in range(j):
            row = row - twice(entry[j, p]) * done[p]
        row = row * twice(scale)
        done.append(row)
        packed = jnp.where(sub_wide == j, row, packed)
    upper[...] = packed
    inv[pl.ds(pl.multiple_of(base, 8), 8), :] = packed[:, TILE:]
    after = pl.multiple_of(jnp.minimum(base + 8, TILE - 8), 8)
    total = mat[pl.ds(after, 8), :]
    for p in range(8):
        weight = jnp.take_along_axis(done[p][:, :TILE], after + sub, axis=1)
        total = total - twice(weight) * done[p]
    tile[...] = total


PASS_ON = (
((1, (1, 0, 0)), (2, (0, -1, 0)), (2, (0, 1, 0)), (4, (1, -1, 0)), (4, (1, 1, 0)), (5, (0, 2, 0)), (7, (1, 2, 0))),
((1, (1, 0, 0)), (1, (1, 0, 1)), (3, (0, -1, 0)), (3, (0, 1, 0)), (4, (0, -1, 1)), (4, (0, 1, 1)), (8, (1, -1, 0)), (8, (1, 1, 0)), (8, (1, -1, 1)), (8, (1, 1, 1)), (9, (0, 2, 0)), (9, (0, 2, 1)), (10, (1, 2, 0)), (10, (1, 2, 1))))


def gather_factor_kernel(
    front, weight_row,
    sibling_rows, high, low, column, top, top_inv, own_panel,
    gathered, corner_in, corner, own_rows, factors, solver, lead, inv, mat, tile, upper, weights,
    local_sem, first_send, first_recv, bulk_send, bulk_recv, row_send, row_recv,
):
    leaf = lax.axis_index("leaf")
    front_id = lax.axis_index("front")
    half = lax.rem(leaf, 2)
    chip = lax.div(front_id, 2)
    core = lax.rem(front_id, 2)
    chips = lax.div(lax.axis_size("front"), 2)
    own, other = half, 1 - half

    def chip_at(offset):
        return lax.rem(chip + offset + chips, chips)

    sibling = (leaf + 1 - 2 * half, front_id)
    right = (leaf, chip_at(1) * 2 + core)
    left = (leaf, chip_at(-1) * 2 + core)
    partner = (leaf, front_id + 1 - 2 * core)
    opposite = (leaf, chip_at(2) * 2 + core)
    sibling_right = (sibling[0], right[1])
    sibling_left = (sibling[0], left[1])
    sibling_opposite = (sibling[0], opposite[1])

    staged = []

    def stage(src, dst, condition=None):
        copy = pltpu.make_async_copy(src, dst, local_sem.at[len(staged)])
        staged.append((condition, copy))
        when(condition, copy.start)

    def when(condition, action):
        if condition is None:
            action()
        else:
            pl.when(condition)(lambda: action())

    def stage_row(r, slot, condition=None):
        rows = pl.ds(r * TILE, TILE)
        for k in range(4):
            stage(front.at[rows, pl.ds(4 * k * TILE, TILE)], slot.at[:, pl.ds(k * TILE, TILE)], condition)
        stage(front.at[rows, pl.ds(TILE, TILE)], slot.at[:, pl.ds(4 * TILE, TILE)], condition)

    corner_slot = corner_in.at[own, pl.ds(pl.multiple_of(chip * TILE, TILE), TILE)]
    for k in range(4):
        stage(front.at[pl.ds(0, TILE), pl.ds(4 * k * TILE, TILE)], corner_slot.at[:, pl.ds(k * TILE, TILE)], core == 0)
    stage_row(0, gathered.at[own, 3 * chip + 1], core == 1)
    stage_row(1, gathered.at[own, 3 * chip + 2 * core])
    for k in range(4):
        stage(front.at[:, pl.ds(4 * k * TILE, TILE)], own_rows.at[:, pl.ds(k * TILE, TILE)])

    stage(weight_row, weights)

    barrier = pltpu.get_barrier_semaphore()
    greeted = (sibling, right, left, opposite, sibling_right, sibling_left, sibling_opposite, partner)
    for device in greeted:
        pl.semaphore_signal(barrier, inc=1, device_id=device, device_id_type=MESH)
    pl.semaphore_wait(barrier, len(greeted))
    for condition, copy in staged:
        when(condition, copy.wait)

    @pl.when((core == 0) & (chip == 0) & (half == 0))
    def _():
        corner_in[0, 0:1, TILE : 2 * TILE] = weights[0:1, 0:TILE]

    sends = []

    def remote(ref, send_sem, recv_sem, device):
        return pltpu.make_async_remote_copy(
            src_ref=ref, dst_ref=ref, send_sem=send_sem, recv_sem=recv_sem, device_id=device, device_id_type=MESH
        )

    def top_pieces(child):
        refs = (corner_in.at[child, pl.ds(0, TILE), pl.ds(0, TILE)], corner_in.at[child, pl.ds(0, 8), pl.ds(TILE, TILE)])
        return [(None, ref, first_recv.at[child, 0, n]) for n, ref in enumerate(refs)]

    def first_pieces(child, offset):
        k = chip_at(offset)
        rows = pl.ds(pl.multiple_of(k * TILE, TILE), TILE)
        return (
            (k >= 1, corner_in.at[child, rows, pl.ds(0, 2 * TILE)], first_recv.at[child, k, 0]),
            (k >= 2, corner_in.at[child, rows, pl.ds(2 * TILE, 2 * TILE)], first_recv.at[child, k, 1]),
        )

    counts = {"top": 0, "pass": 16, "first": 18, 0: 0, 1: 0}

    def start(kind, pool, build, device):
        number = counts[kind]
        counts[kind] += 1

        def make():
            condition, ref, recv_sem = build()
            return condition, remote(ref, pool.at[number], recv_sem, device)

        sends.append((kind, make))
        condition, copy = make()
        when(condition, copy.start)

    def top_send_to(kind, child, devices):
        for device in devices:
            for n in range(2):
                start(kind, first_send, lambda n=n: top_pieces(child)[n], device)

    def top_arrive(child):
        for condition, ref, recv_sem in top_pieces(child):
            remote(ref, first_send.at[0], recv_sem, partner).wait_recv()

    def first_send_to(child, offset, devices, pieces=(0, 1)):
        for device in devices:
            for n in pieces:
                start("first", first_send, lambda n=n: first_pieces(child, offset)[n], device)

    def first_arrive(child, offset):
        for condition, ref, recv_sem in first_pieces(child, offset):
            when(condition, remote(ref, first_send.at[0], recv_sem, partner).wait_recv)

    def bulk_piece(child, offset, from_core, i, q):
        a = 3 * chip_at(offset) + from_core * (1 + i)
        return None, gathered.at[child, a, pl.ds(q * 64, 64)], bulk_recv.at[child, a, q]

    def bulk_send_to(kind, child, offset, i, q, devices):
        for device in devices:
            start(kind, bulk_send, lambda: bulk_piece(child, offset, kind, i, q), device)

    def bulk_arrive(child, offset, from_core, i, q):
        condition, ref, recv_sem = bulk_piece(child, offset, from_core, i, q)
        when(condition, remote(ref, bulk_send.at[0], recv_sem, partner).wait_recv)

    def bulk_step(kind, child, offset, i):
        for q in range(2):
            bulk_arrive(child, offset, kind, i, q)
            if offset == 0:
                onward = (right, left)
            elif offset == -1 and q == 0:
                onward = (right,)
            elif offset == 1 and q == 1:
                onward = (left,)
            else:
                onward = ()
            bulk_send_to(kind, child, offset, i, q, onward + (partner,))

    def own_bulk(kind):
        for i in range(1 + kind):
            for q in range(2):
                bulk_send_to(kind, own, 0, i, q, (sibling, right, left, partner))

    @pl.when((core == 0) & (chip == 0))
    def _():
        top_send_to("top", own, (sibling, right, left, opposite, sibling_right, sibling_left, sibling_opposite, partner))

    @pl.when(core == 0)
    def _():
        first_send_to(own, 0, (sibling, right, left, opposite, partner))
        own_bulk(0)
        first_arrive(other, 0)
        first_send_to(other, 0, (right, left, opposite))

        @pl.when(chip != 0)
        def _():
            top_arrive(own)
            top_send_to("pass", own, (partner,))

        top_arrive(other)
        top_send_to("first", other, (partner,))

    @pl.when(core == 1)
    def _():
        own_bulk(1)
        for child in (own, other):
            top_arrive(child)

    def pass_first():
        @pl.when(core == 0)
        def _():
            first_send_to(other, 0, (partner,))
            for child, offset in ((own, -1), (own, 1), (own, 2), (other, -1), (other, 1), (other, 2)):
                first_arrive(child, offset)
                first_send_to(child, offset, (partner,))

    def last_first():
        @pl.when(core == 1)
        def _():
            for child in (own, other):
                for offset in (0, -1, 1, 2):
                    first_arrive(child, offset)

    def row_copy(r, g):
        return pltpu.make_async_remote_copy(
            src_ref=front.at[pl.ds(r * TILE, TILE), pl.ds((4 * g + 1) * TILE, 3 * TILE)],
            dst_ref=sibling_rows.at[pl.ds(r * TILE, TILE), pl.ds(3 * g * TILE, 3 * TILE)],
            send_sem=row_send.at[r, g],
            recv_sem=row_recv.at[r, g],
            device_id=sibling,
            device_id_type=MESH,
        )

    def start_rows():
        for g in range(4):
            row_copy(1, g).start()

        @pl.when(core == 1)
        def _():
            for g in range(4):
                row_copy(0, g).start()

    def pass_on(point):
        for kind in range(2):
            listed = [step for when_, step in PASS_ON[kind] if when_ == point]
            if listed:

                @pl.when(core == kind)
                def _():
                    for sib, offset, i in listed:
                        bulk_step(kind, other if sib else own, offset, i)

    for k in range(4):
        here = slice(k * TILE, (k + 1) * TILE)
        for child in range(2):
            start_block((corner_in if k == 0 else corner)[child, here, here], mat.at[child], tile.at[child], upper.at[child])

        for part in range(2):

            @pl.loop(part * (TILE // 16), (part + 1) * (TILE // 16))
            def _(step):
                for child in range(2):
                    factor_panel(step, mat.at[child], tile.at[child], upper.at[child], inv.at[child])

            if k == 0:
                (pass_first, last_first)[part]()
            pass_on(2 * k + part)
            if (k, part) == (0, 1):
                start_rows()
                corner[...] = corner_in[...]

        for child in range(2):
            finish_block(k, corner.at[child], inv.at[child], factors.at[child])

    for child in range(2):
        for j in range(3):
            solver[child, j] = right_stack(*halves(factors[child, j]))

    def solve(child, columns):
        one = stack_dot(left_stack(*halves(columns[:, : 2 * TILE])), solver[child, 0])
        one_high, one_low = halves(one)
        two = columns[:, 2 * TILE :] - stack_dot(left_stack(one_high, one_low), solver[child, 2])
        two = stack_dot(left_stack(*halves(two)), solver[child, 1])
        two_high, two_low = halves(two)
        high_low = (jnp.concatenate([one_high, two_high], axis=1), jnp.concatenate([one_low, two_low], axis=1))
        return one, two, high_low

    one, two, _ = solve(own, own_rows[...])
    own_panel[:, : 2 * TILE] = one
    own_panel[:, 2 * TILE :] = two
    pass_on(8)

    @pl.when(core == 1)
    def _():
        for child in (own, other):
            for offset in (0, -1, 1, 2):
                for q in range(2):
                    bulk_arrive(child, offset, 0, 0, q)

    row = lax.broadcasted_iota(jnp.int32, (TILE, TILE), 0)
    col = lax.broadcasted_iota(jnp.int32, (TILE, TILE), 1)
    near = jnp.where(jnp.abs(row - col) == 1, 1.0, 0.0)
    total = jnp.where(row == col, corner_in[0, 0:1, TILE : 2 * TILE] + 4.0, 0.0) - near
    for child in range(2):
        high_low = solve(child, gathered[child, 0, :, : 4 * TILE])[2]
        lead[child] = right_stack(*high_low)
        total = total + (gathered[child, 0, :, 4 * TILE :] - stack_dot(left_stack(*high_low), lead[child]))
    top[...] = total
    start_block(total, mat.at[0], tile.at[0], upper.at[0])

    def panels(child, k):
        rows = pl.ds(3 * k, 3)
        block = gathered[child, rows].reshape(3 * TILE, 5 * TILE)
        whole_high, whole_low = solve(child, block[:, : 4 * TILE])[2]
        high[child, rows] = whole_high.reshape(3, TILE, 4 * TILE)
        low[child, rows] = whole_low.reshape(3, TILE, 4 * TILE)
        product = stack_dot(left_stack(whole_high, whole_low), lead[child])
        column[child, rows] = (block[:, 4 * TILE :] - product).reshape(3, TILE, TILE)

    def partner_rows(*groups):
        @pl.when(core == 0)
        def _():
            for child, offset in groups:
                for i in range(2):
                    for q in range(2):
                        bulk_arrive(child, offset, 1, i, q)

    partner_rows((own, 0), (other, 0))

    @pl.loop(0, 2)
    def _(group):
        for part in range(4):
            factor_panel(4 * group + part, mat.at[0], tile.at[0], upper.at[0], top_inv)
        panels(lax.select(group == 0, own, other), chip)

    pass_on(9)
    partner_rows((own, -1), (own, 1))

    @pl.loop(2, 4)
    def _(group):
        for part in range(4):
            factor_panel(4 * group + part, mat.at[0], tile.at[0], upper.at[0], top_inv)
        panels(own, chip_at(2 * group - 5))

    pass_on(10)
    partner_rows((other, -1), (other, 1))
    for offset in (-1, 1):
        panels(other, chip_at(offset))
    pass_on(11)
    partner_rows((own, 2), (other, 2))
    for child in (own, other):
        panels(child, chip_at(2))

    def sent(kind):
        for name, make in sends:
            if name == kind:
                condition, copy = make()
                when(condition, copy.wait_send)

    @pl.when(core == 0)
    def _():
        sent("first")
        sent(0)

        @pl.when(chip == 0)
        def _():
            sent("top")

        @pl.when(chip != 0)
        def _():
            sent("pass")

    @pl.when(core == 1)
    def _():
        sent(1)

    for g in range(4):
        row_copy(1, g).wait()

    @pl.when(core == 1)
    def _():
        for g in range(4):
            row_copy(0, g).wait()


def finish_block(k, corner, inv, factors):
    here = slice(k * TILE, (k + 1) * TILE)
    inverse = inv[...]
    level, place = divmod(k, 2)
    if place == 0:
        factors[level, 0:TILE, 0:TILE] = inverse
        factors[level, 0:TILE, TILE:] = jnp.zeros((TILE, TILE), f32)
    else:
        before = slice((k - 1) * TILE, k * TILE)
        middle = exact_dot(corner[here, before], factors[level, 0:TILE, 0:TILE], NN)
        factors[level, TILE:, 0:TILE] = -exact_dot(inverse, middle, NN)
        factors[level, TILE:, TILE:] = inverse
    if k < 3:
        rest = slice((k + 1) * TILE, 4 * TILE)
        below = exact_dot(corner[rest, here], inverse, NT)
        corner[rest, here] = below
        corner[rest, rest] -= exact_dot(below, below, NT)
        if level == 0:
            cut = (1 - place) * TILE
            factors[2, :, place * TILE : (place + 1) * TILE] = below[cut:, :]


def gather_factor(front, weights):
    rows, width = front.shape
    local = pl.BlockSpec(memory_space=pltpu.VMEM)
    anywhere = pl.BlockSpec(memory_space=pl.ANY)
    return pl.pallas_call(
        gather_factor_kernel,
        out_shape=(
            jax.ShapeDtypeStruct((rows, 12 * TILE), f32),
            jax.ShapeDtypeStruct((2, 12, TILE, 4 * TILE), bf16),
            jax.ShapeDtypeStruct((2, 12, TILE, 4 * TILE), bf16),
            jax.ShapeDtypeStruct((2, 12, TILE, TILE), f32),
            jax.ShapeDtypeStruct((TILE, TILE), f32),
            jax.ShapeDtypeStruct((TILE, TILE), f32),
            jax.ShapeDtypeStruct((rows, 4 * TILE), f32),
        ),
        in_specs=[pl.BlockSpec(memory_space=pltpu.HBM), pl.BlockSpec(memory_space=pltpu.HBM)],
        out_specs=(anywhere, local, local, local, local, local, local),
        scratch_shapes=[
            pltpu.VMEM((2, 12, TILE, 5 * TILE), f32),
            pltpu.VMEM((2, 4 * TILE, 4 * TILE), f32),
            pltpu.VMEM((2, 4 * TILE, 4 * TILE), f32),
            pltpu.VMEM((rows, 4 * TILE), f32),
            pltpu.VMEM((2, 3, 2 * TILE, 2 * TILE), f32),
            pltpu.VMEM((2, 3, 2 * TILE, 6 * TILE), bf16),
            pltpu.VMEM((2, TILE, 12 * TILE), bf16),
            pltpu.VMEM((2, TILE, TILE), f32),
            pltpu.VMEM((2, TILE, 2 * TILE), f32),
            pltpu.VMEM((2, 8, 2 * TILE), f32),
            pltpu.VMEM((2, 8, 2 * TILE), f32),
            pltpu.VMEM((1, 2 * TILE), f32),
            pltpu.SemaphoreType.DMA((20,)),
            pltpu.SemaphoreType.DMA((60,)),
            pltpu.SemaphoreType.DMA((2, 4, 2)),
            pltpu.SemaphoreType.DMA((80,)),
            pltpu.SemaphoreType.DMA((2, 12, 2)),
            pltpu.SemaphoreType.DMA((2, 4)),
            pltpu.SemaphoreType.DMA((2, 4)),
        ],
        compiler_params=pltpu.CompilerParams(
            collective_id=0, has_side_effects=True, vmem_limit_bytes=34 * 2**20
        ),
        name="gather_factor",
    )(front, weights)


def assemble_kernel(
    index, front, sibling_rows, weight_row, high, low, column, top, top_inv, own_panel,
    leaf_panel, parent_panel, parent_update,
    own_front, sib_front, parent, parent_high, parent_low, weights, child_of, row_sem,
):
    leaf = lax.axis_index("leaf")
    front_id = lax.axis_index("front")
    half = lax.rem(leaf, 2)
    first = leaf - half
    row_loads = [
        pltpu.make_async_copy(front, own_front, row_sem.at[0]),
        pltpu.make_async_copy(sibling_rows, sib_front, row_sem.at[1]),
        pltpu.make_async_copy(weight_row, weights, row_sem.at[2]),
    ]
    for copy in row_loads:
        copy.start()
    leaf_panel[...] = own_panel[...]

    @pl.loop(0, 32)
    def _(p):
        child_of[0, p] = -1
        child_of[1, p] = -1

    for child in range(2):
        for a in range(12):
            child_of[child, index[a, 0, first + child]] = a

    row = lax.broadcasted_iota(jnp.int32, (TILE, TILE), 0)
    col = lax.broadcasted_iota(jnp.int32, (TILE, TILE), 1)
    near = jnp.where(jnp.abs(row - col) == 1, 1.0, 0.0)
    above = jnp.where((row == 0) & (col == TILE - 1), 1.0, 0.0)
    under = jnp.where((row == TILE - 1) & (col == 0), 1.0, 0.0)

    @pl.loop(0, 32)
    def _(p):
        total = jnp.zeros((TILE, TILE), f32)
        for child in range(2):
            a = child_of[child, p]
            total = total + jnp.where(a >= 0, column[child, jnp.maximum(a, 0)], 0.0)
        parent[p] = total

    parent[0] = top[...]
    parent[1] -= above

    last = right_stack(*halves(top_inv[...]))
    for q in range(8):
        block = parent[4 * q : 4 * q + 4].reshape(4 * TILE, TILE)
        done = stack_dot(left_stack(*halves(block)), last)
        parent[4 * q : 4 * q + 4] = done.reshape(4, TILE, TILE)
        done_high, done_low = halves(done)
        parent_high[4 * q * TILE : 4 * (q + 1) * TILE, :] = done_high
        parent_low[4 * q * TILE : 4 * (q + 1) * TILE, :] = done_low

    place = 4 * front_id + 2 * half
    parent_panel[...] = parent[pl.ds(place, 2)].reshape(2 * TILE, TILE)
    here = pl.ds(pl.multiple_of(place * TILE, TILE), 2 * TILE)
    mine = left_stack(parent_high[here, :], parent_low[here, :])
    for start in range(TILE, 32 * TILE, 4 * TILE):
        stop = min(start + 4 * TILE, 32 * TILE)
        there = right_stack(parent_high[start:stop, :], parent_low[start:stop, :])
        parent_update[:, start - TILE : stop - TILE] = -stack_dot(mine, there)

    def columns_of(p):
        return pl.ds(pl.multiple_of((p - 1) * TILE, TILE), TILE)

    for copy in row_loads:
        copy.wait()
    for kin in range(2):
        child = half if kin == 0 else 1 - half
        source = own_front if kin == 0 else sib_front
        for r in range(2):
            a = child_of[child, place + r]
            rows = pl.ds(r * TILE, TILE)

            @pl.when(a >= 0)
            def _():
                local = 4 * lax.div(a, 3) + lax.rem(a, 3) + 1 - 2 * front_id
                source_rows = pl.ds(pl.multiple_of(local * TILE, TILE), TILE)
                lead = left_stack(high[child, a], low[child, a])
                for g in range(4):
                    others = right_stack(
                        high[child, pl.ds(3 * g, 3)].reshape(3 * TILE, 4 * TILE),
                        low[child, pl.ds(3 * g, 3)].reshape(3 * TILE, 4 * TILE),
                    )
                    product = stack_dot(lead, others)
                    for m in range(3):
                        b = 3 * g + m
                        p = index[b, 0, first + child]
                        t = 4 * g + m + 1 if kin == 0 else b
                        value = source[source_rows, t * TILE : (t + 1) * TILE] - product[:, m * TILE : (m + 1) * TILE]
                        if b == 0:
                            continue
                        parent_update[rows, columns_of(p)] += value

    for r in range(2):
        p = place + r
        rows = slice(r * TILE, (r + 1) * TILE)
        own_weights = weights[0:1, r * TILE : (r + 1) * TILE]
        inside = p < SEP2_TILES

        @pl.when(p >= 1)
        def _():
            extra = jnp.where(inside, 1.0, 0.0)
            parent_update[rows, columns_of(p)] += jnp.where(row == col, own_weights + 4.0 * extra, 0.0) - near * extra

        @pl.when((p >= 2) & inside)
        def _():
            parent_update[rows, columns_of(p - 1)] -= above

        @pl.when(p + 1 < SEP2_TILES)
        def _():
            parent_update[rows, columns_of(p + 1)] -= under


def assemble(index, front, weights, sibling_rows, *rest):
    rows, width = front.shape
    anywhere = pl.BlockSpec(memory_space=pl.ANY)
    local = pl.BlockSpec(memory_space=pltpu.VMEM)
    return pl.pallas_call(
        assemble_kernel,
        out_shape=(
            jax.ShapeDtypeStruct((rows, 4 * TILE), f32),
            jax.ShapeDtypeStruct((rows, TILE), f32),
            jax.ShapeDtypeStruct((rows, 31 * TILE), f32),
        ),
        in_specs=[pl.BlockSpec(memory_space=pltpu.SMEM), pl.BlockSpec(memory_space=pltpu.HBM), anywhere]
        + [pl.BlockSpec(memory_space=pltpu.HBM)]
        + [local] * 6,
        out_specs=(local, local, local),
        scratch_shapes=[
            pltpu.VMEM((rows, width), f32),
            pltpu.VMEM((rows, 12 * TILE), f32),
            pltpu.VMEM((32, TILE, TILE), f32),
            pltpu.VMEM((32 * TILE, TILE), bf16),
            pltpu.VMEM((32 * TILE, TILE), bf16),
            pltpu.VMEM((1, 2 * TILE), f32),
            pltpu.SMEM((2, 32), jnp.int32),
            pltpu.SemaphoreType.DMA((3,)),
        ],
        compiler_params=pltpu.CompilerParams(vmem_limit_bytes=30 * 2**20),
        name="assemble",
    )(index, front, sibling_rows, weights, *rest)


def on_device(leaf_fronts, screen_weights, parent_tile_index):
    front = leaf_fronts[0, 0]
    weights = screen_weights[0]
    index = parent_tile_index.transpose(2, 1, 0)
    front = pltpu.with_memory_space_constraint(front, pltpu.HBM)
    weights = pltpu.with_memory_space_constraint(weights, pltpu.HBM)
    leaf_panel, parent_panel, parent_update = assemble(index, front, weights, *gather_factor(front, weights))
    return leaf_panel[None, None], parent_panel[None, None], parent_update[None, None]


def solution(mesh):
    rows = P("leaf", None, "front", None)
    return jax.shard_map(
        on_device,
        mesh=mesh,
        in_specs=(rows, P("leaf", None, "front"), P()),
        out_specs=(rows, rows, rows),
        check_vma=False,
    )
```

```python
import functools

import jax
import jax.numpy as jnp
from jax import lax
from jax.experimental import pallas as pl
from jax.experimental.pallas import tpu as pltpu
from jax.sharding import PartitionSpec as P

MESH = pl.DeviceIdType.MESH
HIGHEST = lax.Precision.HIGHEST
NT = (((1,), (1,)), ((), ()))
NN = (((1,), (0,)), ((), ()))
TN = (((0,), (0,)), ((), ()))
TILE = 128
SEP2_TILES = 8
f32 = jnp.float32
bf16 = jnp.bfloat16


def exact_dot(a, b, dims):
    return lax.dot_general(a, b, dims, precision=HIGHEST, preferred_element_type=f32)


def thirds(x):
    high = x.astype(bf16)
    rest = x - high.astype(f32)
    mid = rest.astype(bf16)
    low = (rest - mid.astype(f32)).astype(bf16)
    return high, mid, low


def halves(x):
    high = x.astype(bf16)
    return high, (x - high.astype(f32)).astype(bf16)


def left_stack(high, low):
    return jnp.concatenate([high, low, high], axis=1)


def right_stack(high, low):
    return jnp.concatenate([high, high, low], axis=1)


def stack_dot(left, right):
    return lax.dot_general(left, right, NT, preferred_element_type=f32)


def start_block(block, mat, tile, upper):
    row = lax.broadcasted_iota(jnp.int32, (TILE, TILE), 0)
    col = lax.broadcasted_iota(jnp.int32, (TILE, TILE), 1)
    mat[:, :TILE] = block
    mat[:, TILE:] = (row == col).astype(f32)
    tile[...] = mat[0:8, :]
    upper[...] = jnp.zeros_like(upper)


def twice(x):
    return jnp.concatenate([x, x], axis=1)


def factor_panel(step, mat, tile, upper, inv):
    base = step * 8
    sub = lax.broadcasted_iota(jnp.int32, (8, TILE), 0)
    sub_wide = lax.broadcasted_iota(jnp.int32, (8, 2 * TILE), 0)
    high, mid, low = thirds(upper[...])
    left = jnp.concatenate([high, high, mid, high, low, mid], axis=0)[:, :TILE]
    right = jnp.concatenate([high, mid, high, low, high, mid], axis=0)
    mat[...] -= lax.dot_general(left, right, TN, preferred_element_type=f32)
    rows = tile[...]
    cols = [
        jnp.take_along_axis(rows[:, :TILE], jnp.full((8, TILE), base + j, jnp.int32), axis=1) for j in range(8)
    ]
    done = []
    packed = jnp.zeros((8, 2 * TILE), f32)
    entry = {}
    for j in range(8):
        scale = lax.rsqrt(jnp.broadcast_to(cols[j][j : j + 1, :], (8, TILE)))
        column = cols[j] * scale
        for k in range(j + 1, 8):
            entry[k, j] = jnp.broadcast_to(column[k : k + 1, :], (8, TILE))
            cols[k] = cols[k] - column * entry[k, j]
        row = jnp.broadcast_to(rows[j : j + 1, :], (8, 2 * TILE))
        for p in range(j):
            row = row - twice(entry[j, p]) * done[p]
        row = row * twice(scale)
        done.append(row)
        packed = jnp.where(sub_wide == j, row, packed)
    upper[...] = packed
    inv[pl.ds(pl.multiple_of(base, 8), 8), :] = packed[:, TILE:]
    after = pl.multiple_of(jnp.minimum(base + 8, TILE - 8), 8)
    total = mat[pl.ds(after, 8), :]
    for p in range(8):
        weight = jnp.take_along_axis(done[p][:, :TILE], after + sub, axis=1)
        total = total - twice(weight) * done[p]
    tile[...] = total


PASS_ON = (
    (
        (3, (1, 0, 0)),
        (4, (0, -1, 0)), (4, (0, 1, 0)),
        (8, (1, -1, 0)), (8, (1, 1, 0)),
        (9, (0, 2, 0)),
        (12, (1, 2, 0)),
    ),
    (
        (4, (1, 0, 0)), (4, (1, 0, 1)),
        (7, (0, -1, 0)), (7, (0, 1, 0)),
        (8, (0, -1, 1)), (8, (0, 1, 1)),
        (14, (1, -1, 0)), (14, (1, 1, 0)),
        (15, (1, -1, 1)), (15, (1, 1, 1)),
        (19, (0, 2, 0)), (19, (0, 2, 1)),
        (21, (1, 2, 0)), (21, (1, 2, 1)),
    ),
)
ROW_POINT = 1


def gather_factor_kernel(
    front, weight_row,
    sibling_rows, high, low, column, top, top_inv, own_panel,
    gathered, corner_in, corner, own_rows, factors, solver, lead, inv, mat, tile, upper, weights,
    local_sem, first_send, first_recv, bulk_send, bulk_recv, row_send, row_recv,
):
    leaf = lax.axis_index("leaf")
    front_id = lax.axis_index("front")
    half = lax.rem(leaf, 2)
    chip = lax.div(front_id, 2)
    core = lax.rem(front_id, 2)
    chips = lax.div(lax.axis_size("front"), 2)
    own, other = half, 1 - half

    def chip_at(offset):
        return lax.rem(chip + offset + chips, chips)

    sibling = (leaf + 1 - 2 * half, front_id)
    right = (leaf, chip_at(1) * 2 + core)
    left = (leaf, chip_at(-1) * 2 + core)
    partner = (leaf, front_id + 1 - 2 * core)
    opposite = (leaf, chip_at(2) * 2 + core)
    sibling_right = (sibling[0], right[1])
    sibling_left = (sibling[0], left[1])
    sibling_opposite = (sibling[0], opposite[1])

    staged = []

    def stage(src, dst, condition=None):
        copy = pltpu.make_async_copy(src, dst, local_sem.at[len(staged)])
        staged.append((condition, copy))
        when(condition, copy.start)

    def when(condition, action):
        if condition is None:
            action()
        else:
            pl.when(condition)(lambda: action())

    def stage_row(r, slot, condition=None):
        rows = pl.ds(r * TILE, TILE)
        for k in range(4):
            stage(front.at[rows, pl.ds(4 * k * TILE, TILE)], slot.at[:, pl.ds(k * TILE, TILE)], condition)
        stage(front.at[rows, pl.ds(TILE, TILE)], slot.at[:, pl.ds(4 * TILE, TILE)], condition)

    corner_slot = corner_in.at[own, pl.ds(pl.multiple_of(chip * TILE, TILE), TILE)]
    for k in range(4):
        stage(front.at[pl.ds(0, TILE), pl.ds(4 * k * TILE, TILE)], corner_slot.at[:, pl.ds(k * TILE, TILE)], core == 0)
    stage_row(0, gathered.at[own, 3 * chip + 1], core == 1)
    stage_row(1, gathered.at[own, 3 * chip + 2 * core])
    for k in range(4):
        stage(front.at[:, pl.ds(4 * k * TILE, TILE)], own_rows.at[:, pl.ds(k * TILE, TILE)])

    stage(weight_row, weights)

    barrier = pltpu.get_barrier_semaphore()
    greeted = (sibling, right, left, opposite, sibling_right, sibling_left, sibling_opposite, partner)
    for device in greeted:
        pl.semaphore_signal(barrier, inc=1, device_id=device, device_id_type=MESH)
    pl.semaphore_wait(barrier, len(greeted))
    for condition, copy in staged:
        when(condition, copy.wait)

    @pl.when((core == 0) & (chip == 0) & (half == 0))
    def _():
        corner_in[0, 0:1, TILE : 2 * TILE] = weights[0:1, 0:TILE]

    sends = []

    def remote(ref, send_sem, recv_sem, device):
        return pltpu.make_async_remote_copy(
            src_ref=ref, dst_ref=ref, send_sem=send_sem, recv_sem=recv_sem, device_id=device, device_id_type=MESH
        )

    def top_pieces(child):
        refs = (corner_in.at[child, pl.ds(0, TILE), pl.ds(0, TILE)], corner_in.at[child, pl.ds(0, 8), pl.ds(TILE, TILE)])
        return [(None, ref, first_recv.at[child, 0, n]) for n, ref in enumerate(refs)]

    def first_pieces(child, offset):
        k = chip_at(offset)
        rows = pl.ds(pl.multiple_of(k * TILE, TILE), TILE)
        return (
            (k >= 1, corner_in.at[child, rows, pl.ds(0, 2 * TILE)], first_recv.at[child, k, 0]),
            (k >= 2, corner_in.at[child, rows, pl.ds(2 * TILE, 2 * TILE)], first_recv.at[child, k, 1]),
        )

    counts = {"top": 0, "pass": 16, "first": 18, 0: 0, 1: 0}

    def start(kind, pool, build, device):
        number = counts[kind]
        counts[kind] += 1

        def make():
            condition, ref, recv_sem = build()
            return condition, remote(ref, pool.at[number], recv_sem, device)

        sends.append((kind, make))
        condition, copy = make()
        when(condition, copy.start)

    def top_send_to(kind, child, devices):
        for device in devices:
            for n in range(2):
                start(kind, first_send, lambda n=n: top_pieces(child)[n], device)

    def top_arrive(child):
        for condition, ref, recv_sem in top_pieces(child):
            remote(ref, first_send.at[0], recv_sem, partner).wait_recv()

    def first_send_to(child, offset, devices, pieces=(0, 1)):
        for device in devices:
            for n in pieces:
                start("first", first_send, lambda n=n: first_pieces(child, offset)[n], device)

    def first_arrive(child, offset):
        for condition, ref, recv_sem in first_pieces(child, offset):
            when(condition, remote(ref, first_send.at[0], recv_sem, partner).wait_recv)

    def bulk_piece(child, offset, from_core, i, q):
        a = 3 * chip_at(offset) + from_core * (1 + i)
        return None, gathered.at[child, a, pl.ds(q * 64, 64)], bulk_recv.at[child, a, q]

    def bulk_send_to(kind, child, offset, i, q, devices):
        for device in devices:
            start(kind, bulk_send, lambda: bulk_piece(child, offset, kind, i, q), device)

    def bulk_arrive(child, offset, from_core, i, q):
        condition, ref, recv_sem = bulk_piece(child, offset, from_core, i, q)
        when(condition, remote(ref, bulk_send.at[0], recv_sem, partner).wait_recv)

    def bulk_step(kind, child, offset, i):
        for q in range(2):
            bulk_arrive(child, offset, kind, i, q)
            if offset == 0:
                onward = (right, left)
            elif offset == -1 and q == 0:
                onward = (right,)
            elif offset == 1 and q == 1:
                onward = (left,)
            else:
                onward = ()
            bulk_send_to(kind, child, offset, i, q, onward + (partner,))

    def own_bulk(kind):
        for i in range(1 + kind):
            for q in range(2):
                bulk_send_to(kind, own, 0, i, q, (sibling, right, left, partner))

    @pl.when((core == 0) & (chip == 0))
    def _():
        top_send_to("top", own, (sibling, right, left, opposite, sibling_right, sibling_left, sibling_opposite, partner))

    @pl.when(core == 0)
    def _():
        first_send_to(own, 0, (sibling, right, left, opposite, partner))
        own_bulk(0)
        first_arrive(other, 0)
        first_send_to(other, 0, (right, left, opposite))

        @pl.when(chip != 0)
        def _():
            top_arrive(own)
            top_send_to("pass", own, (partner,))

        top_arrive(other)
        top_send_to("first", other, (partner,))

    @pl.when(core == 1)
    def _():
        own_bulk(1)
        for child in (own, other):
            top_arrive(child)

    def pass_first():
        @pl.when(core == 0)
        def _():
            first_send_to(other, 0, (partner,))
            for child, offset in ((own, -1), (own, 1), (own, 2), (other, -1), (other, 1), (other, 2)):
                first_arrive(child, offset)
                first_send_to(child, offset, (partner,))

    def last_first():
        @pl.when(core == 1)
        def _():
            for child in (own, other):
                for offset in (0, -1, 1, 2):
                    first_arrive(child, offset)

    def row_copy(r, g):
        return pltpu.make_async_remote_copy(
            src_ref=front.at[pl.ds(r * TILE, TILE), pl.ds((4 * g + 1) * TILE, 3 * TILE)],
            dst_ref=sibling_rows.at[pl.ds(r * TILE, TILE), pl.ds(3 * g * TILE, 3 * TILE)],
            send_sem=row_send.at[r, g],
            recv_sem=row_recv.at[r, g],
            device_id=sibling,
            device_id_type=MESH,
        )

    def start_rows():
        for g in range(4):
            row_copy(1, g).start()

        @pl.when(core == 1)
        def _():
            for g in range(4):
                row_copy(0, g).start()

    def pass_on(point):
        for kind in range(2):
            listed = [step for when_, step in PASS_ON[kind] if when_ == point]
            if listed:

                @pl.when(core == kind)
                def _():
                    for sib, offset, i in listed:
                        bulk_step(kind, other if sib else own, offset, i)

    for k in range(4):
        here = slice(k * TILE, (k + 1) * TILE)
        for child in range(2):
            start_block((corner_in if k == 0 else corner)[child, here, here], mat.at[child], tile.at[child], upper.at[child])

        for part in range(4):

            @pl.loop(part * (TILE // 32), (part + 1) * (TILE // 32))
            def _(step):
                for child in range(2):
                    factor_panel(step, mat.at[child], tile.at[child], upper.at[child], inv.at[child])

            if (k, part) == (0, 1):
                pass_first()
            if (k, part) == (0, 3):
                last_first()
                corner[...] = corner_in[...]
            pass_on(4 * k + part)
            if 4 * k + part == ROW_POINT:
                start_rows()

        for child in range(2):
            finish_block(k, corner.at[child], inv.at[child], factors.at[child])

    for child in range(2):
        for j in range(3):
            solver[child, j] = right_stack(*halves(factors[child, j]))

    def solve(child, columns):
        one = stack_dot(left_stack(*halves(columns[:, : 2 * TILE])), solver[child, 0])
        one_high, one_low = halves(one)
        two = columns[:, 2 * TILE :] - stack_dot(left_stack(one_high, one_low), solver[child, 2])
        two = stack_dot(left_stack(*halves(two)), solver[child, 1])
        two_high, two_low = halves(two)
        high_low = (jnp.concatenate([one_high, two_high], axis=1), jnp.concatenate([one_low, two_low], axis=1))
        return one, two, high_low

    pass_on(16)
    one, two, _ = solve(own, own_rows[...])
    own_panel[:, : 2 * TILE] = one
    own_panel[:, 2 * TILE :] = two
    pass_on(17)

    @pl.when(core == 1)
    def _():
        for child in (own, other):
            for offset in (0, -1, 1, 2):
                for q in range(2):
                    bulk_arrive(child, offset, 0, 0, q)

    row = lax.broadcasted_iota(jnp.int32, (TILE, TILE), 0)
    col = lax.broadcasted_iota(jnp.int32, (TILE, TILE), 1)
    near = jnp.where(jnp.abs(row - col) == 1, 1.0, 0.0)
    total = jnp.where(row == col, corner_in[0, 0:1, TILE : 2 * TILE] + 4.0, 0.0) - near
    for child in range(2):
        high_low = solve(child, gathered[child, 0, :, : 4 * TILE])[2]
        lead[child] = right_stack(*high_low)
        total = total + (gathered[child, 0, :, 4 * TILE :] - stack_dot(left_stack(*high_low), lead[child]))
    top[...] = total
    start_block(total, mat.at[0], tile.at[0], upper.at[0])

    def panels(child, k):
        rows = pl.ds(3 * k, 3)
        block = gathered[child, rows].reshape(3 * TILE, 5 * TILE)
        whole_high, whole_low = solve(child, block[:, : 4 * TILE])[2]
        high[child, rows] = whole_high.reshape(3, TILE, 4 * TILE)
        low[child, rows] = whole_low.reshape(3, TILE, 4 * TILE)
        product = stack_dot(left_stack(whole_high, whole_low), lead[child])
        column[child, rows] = (block[:, 4 * TILE :] - product).reshape(3, TILE, TILE)

    def partner_rows(*groups):
        @pl.when(core == 0)
        def _():
            for child, offset in groups:
                for i in range(2):
                    for q in range(2):
                        bulk_arrive(child, offset, 1, i, q)

    pairs = (((own, 0), (other, 0)), ((own, -1), (own, 1)), ((other, -1), (other, 1)), ((own, 2), (other, 2)))

    @pl.loop(0, 4)
    def _(pair):
        for number in range(4):

            @pl.when(pair == number)
            def _():
                pass_on(18 + number)
                partner_rows(*pairs[number])

        panels(lax.select(pair == 2, other, own), chip_at(lax.select(pair == 0, 0, lax.select(pair == 3, 2, -1))))
        panels(lax.select(pair == 1, own, other), chip_at(lax.select(pair == 0, 0, lax.select(pair == 3, 2, 1))))
        for part in range(4):
            factor_panel(4 * pair + part, mat.at[0], tile.at[0], upper.at[0], top_inv)

    def sent(kind):
        for name, make in sends:
            if name == kind:
                condition, copy = make()
                when(condition, copy.wait_send)

    @pl.when(core == 0)
    def _():
        sent("first")
        sent(0)

        @pl.when(chip == 0)
        def _():
            sent("top")

        @pl.when(chip != 0)
        def _():
            sent("pass")

    @pl.when(core == 1)
    def _():
        sent(1)

    for g in range(4):
        row_copy(1, g).wait()

    @pl.when(core == 1)
    def _():
        for g in range(4):
            row_copy(0, g).wait()


def finish_block(k, corner, inv, factors):
    here = slice(k * TILE, (k + 1) * TILE)
    inverse = inv[...]
    level, place = divmod(k, 2)
    if place == 0:
        factors[level, 0:TILE, 0:TILE] = inverse
        factors[level, 0:TILE, TILE:] = jnp.zeros((TILE, TILE), f32)
    else:
        before = slice((k - 1) * TILE, k * TILE)
        middle = exact_dot(corner[here, before], factors[level, 0:TILE, 0:TILE], NN)
        factors[level, TILE:, 0:TILE] = -exact_dot(inverse, middle, NN)
        factors[level, TILE:, TILE:] = inverse
    if k < 3:
        rest = slice((k + 1) * TILE, 4 * TILE)
        below = exact_dot(corner[rest, here], inverse, NT)
        corner[rest, here] = below
        corner[rest, rest] -= exact_dot(below, below, NT)
        if level == 0:
            cut = (1 - place) * TILE
            factors[2, :, place * TILE : (place + 1) * TILE] = below[cut:, :]


def gather_factor(front, weights):
    rows, width = front.shape
    local = pl.BlockSpec(memory_space=pltpu.VMEM)
    anywhere = pl.BlockSpec(memory_space=pl.ANY)
    return pl.pallas_call(
        gather_factor_kernel,
        out_shape=(
            jax.ShapeDtypeStruct((rows, 12 * TILE), f32),
            jax.ShapeDtypeStruct((2, 12, TILE, 4 * TILE), bf16),
            jax.ShapeDtypeStruct((2, 12, TILE, 4 * TILE), bf16),
            jax.ShapeDtypeStruct((2, 12, TILE, TILE), f32),
            jax.ShapeDtypeStruct((TILE, TILE), f32),
            jax.ShapeDtypeStruct((TILE, TILE), f32),
            jax.ShapeDtypeStruct((rows, 4 * TILE), f32),
        ),
        in_specs=[pl.BlockSpec(memory_space=pltpu.HBM), pl.BlockSpec(memory_space=pltpu.HBM)],
        out_specs=(anywhere, local, local, local, local, local, local),
        scratch_shapes=[
            pltpu.VMEM((2, 12, TILE, 5 * TILE), f32),
            pltpu.VMEM((2, 4 * TILE, 4 * TILE), f32),
            pltpu.VMEM((2, 4 * TILE, 4 * TILE), f32),
            pltpu.VMEM((rows, 4 * TILE), f32),
            pltpu.VMEM((2, 3, 2 * TILE, 2 * TILE), f32),
            pltpu.VMEM((2, 3, 2 * TILE, 6 * TILE), bf16),
            pltpu.VMEM((2, TILE, 12 * TILE), bf16),
            pltpu.VMEM((2, TILE, TILE), f32),
            pltpu.VMEM((2, TILE, 2 * TILE), f32),
            pltpu.VMEM((2, 8, 2 * TILE), f32),
            pltpu.VMEM((2, 8, 2 * TILE), f32),
            pltpu.VMEM((1, 2 * TILE), f32),
            pltpu.SemaphoreType.DMA((20,)),
            pltpu.SemaphoreType.DMA((60,)),
            pltpu.SemaphoreType.DMA((2, 4, 2)),
            pltpu.SemaphoreType.DMA((80,)),
            pltpu.SemaphoreType.DMA((2, 12, 2)),
            pltpu.SemaphoreType.DMA((2, 4)),
            pltpu.SemaphoreType.DMA((2, 4)),
        ],
        compiler_params=pltpu.CompilerParams(
            collective_id=0, has_side_effects=True, vmem_limit_bytes=34 * 2**20
        ),
        name="gather_factor",
    )(front, weights)


def assemble_kernel(
    index, front, sibling_rows, weight_row, high, low, column, top, top_inv, own_panel,
    leaf_panel, parent_panel, parent_update,
    own_front, sib_front, parent, parent_high, parent_low, weights, child_of, row_sem,
):
    leaf = lax.axis_index("leaf")
    front_id = lax.axis_index("front")
    half = lax.rem(leaf, 2)
    first = leaf - half
    row_loads = [
        pltpu.make_async_copy(front, own_front, row_sem.at[0]),
        pltpu.make_async_copy(sibling_rows, sib_front, row_sem.at[1]),
        pltpu.make_async_copy(weight_row, weights, row_sem.at[2]),
    ]
    for copy in row_loads:
        copy.start()
    leaf_panel[...] = own_panel[...]

    @pl.loop(0, 32)
    def _(p):
        child_of[0, p] = -1
        child_of[1, p] = -1

    for child in range(2):
        for a in range(12):
            child_of[child, index[a, 0, first + child]] = a

    row = lax.broadcasted_iota(jnp.int32, (TILE, TILE), 0)
    col = lax.broadcasted_iota(jnp.int32, (TILE, TILE), 1)
    near = jnp.where(jnp.abs(row - col) == 1, 1.0, 0.0)
    above = jnp.where((row == 0) & (col == TILE - 1), 1.0, 0.0)
    under = jnp.where((row == TILE - 1) & (col == 0), 1.0, 0.0)

    @pl.loop(0, 32)
    def _(p):
        total = jnp.zeros((TILE, TILE), f32)
        for child in range(2):
            a = child_of[child, p]
            total = total + jnp.where(a >= 0, column[child, jnp.maximum(a, 0)], 0.0)
        parent[p] = total

    parent[0] = top[...]
    parent[1] -= above

    last = right_stack(*halves(top_inv[...]))
    for q in range(8):
        block = parent[4 * q : 4 * q + 4].reshape(4 * TILE, TILE)
        done = stack_dot(left_stack(*halves(block)), last)
        parent[4 * q : 4 * q + 4] = done.reshape(4, TILE, TILE)
        done_high, done_low = halves(done)
        parent_high[4 * q * TILE : 4 * (q + 1) * TILE, :] = done_high
        parent_low[4 * q * TILE : 4 * (q + 1) * TILE, :] = done_low

    place = 4 * front_id + 2 * half
    parent_panel[...] = parent[pl.ds(place, 2)].reshape(2 * TILE, TILE)
    here = pl.ds(pl.multiple_of(place * TILE, TILE), 2 * TILE)
    mine = left_stack(parent_high[here, :], parent_low[here, :])
    for start in range(TILE, 32 * TILE, 4 * TILE):
        stop = min(start + 4 * TILE, 32 * TILE)
        there = right_stack(parent_high[start:stop, :], parent_low[start:stop, :])
        parent_update[:, start - TILE : stop - TILE] = -stack_dot(mine, there)

    def columns_of(p):
        return pl.ds(pl.multiple_of((p - 1) * TILE, TILE), TILE)

    for copy in row_loads:
        copy.wait()
    for kin in range(2):
        child = half if kin == 0 else 1 - half
        source = own_front if kin == 0 else sib_front
        for r in range(2):
            a = child_of[child, place + r]
            rows = pl.ds(r * TILE, TILE)

            @pl.when(a >= 0)
            def _():
                local = 4 * lax.div(a, 3) + lax.rem(a, 3) + 1 - 2 * front_id
                source_rows = pl.ds(pl.multiple_of(local * TILE, TILE), TILE)
                lead = left_stack(high[child, a], low[child, a])
                for g in range(4):
                    others = right_stack(
                        high[child, pl.ds(3 * g, 3)].reshape(3 * TILE, 4 * TILE),
                        low[child, pl.ds(3 * g, 3)].reshape(3 * TILE, 4 * TILE),
                    )
                    product = stack_dot(lead, others)
                    for m in range(3):
                        b = 3 * g + m
                        p = index[b, 0, first + child]
                        t = 4 * g + m + 1 if kin == 0 else b
                        value = source[source_rows, t * TILE : (t + 1) * TILE] - product[:, m * TILE : (m + 1) * TILE]
                        if b == 0:
                            continue
                        parent_update[rows, columns_of(p)] += value

    for r in range(2):
        p = place + r
        rows = slice(r * TILE, (r + 1) * TILE)
        own_weights = weights[0:1, r * TILE : (r + 1) * TILE]
        inside = p < SEP2_TILES

        @pl.when(p >= 1)
        def _():
            extra = jnp.where(inside, 1.0, 0.0)
            parent_update[rows, columns_of(p)] += jnp.where(row == col, own_weights + 4.0 * extra, 0.0) - near * extra

        @pl.when((p >= 2) & inside)
        def _():
            parent_update[rows, columns_of(p - 1)] -= above

        @pl.when(p + 1 < SEP2_TILES)
        def _():
            parent_update[rows, columns_of(p + 1)] -= under


def assemble(index, front, weights, sibling_rows, *rest):
    rows, width = front.shape
    anywhere = pl.BlockSpec(memory_space=pl.ANY)
    local = pl.BlockSpec(memory_space=pltpu.VMEM)
    return pl.pallas_call(
        assemble_kernel,
        out_shape=(
            jax.ShapeDtypeStruct((rows, 4 * TILE), f32),
            jax.ShapeDtypeStruct((rows, TILE), f32),
            jax.ShapeDtypeStruct((rows, 31 * TILE), f32),
        ),
        in_specs=[pl.BlockSpec(memory_space=pltpu.SMEM), pl.BlockSpec(memory_space=pltpu.HBM), anywhere]
        + [pl.BlockSpec(memory_space=pltpu.HBM)]
        + [local] * 6,
        out_specs=(local, local, local),
        scratch_shapes=[
            pltpu.VMEM((rows, width), f32),
            pltpu.VMEM((rows, 12 * TILE), f32),
            pltpu.VMEM((32, TILE, TILE), f32),
            pltpu.VMEM((32 * TILE, TILE), bf16),
            pltpu.VMEM((32 * TILE, TILE), bf16),
            pltpu.VMEM((1, 2 * TILE), f32),
            pltpu.SMEM((2, 32), jnp.int32),
            pltpu.SemaphoreType.DMA((3,)),
        ],
        compiler_params=pltpu.CompilerParams(vmem_limit_bytes=30 * 2**20),
        name="assemble",
    )(index, front, sibling_rows, weights, *rest)


def on_device(leaf_fronts, screen_weights, parent_tile_index):
    front = leaf_fronts[0, 0]
    weights = screen_weights[0]
    index = parent_tile_index.transpose(2, 1, 0)
    front = pltpu.with_memory_space_constraint(front, pltpu.HBM)
    weights = pltpu.with_memory_space_constraint(weights, pltpu.HBM)
    leaf_panel, parent_panel, parent_update = assemble(index, front, weights, *gather_factor(front, weights))
    return leaf_panel[None, None], parent_panel[None, None], parent_update[None, None]


def solution(mesh):
    rows = P("leaf", None, "front", None)
    return jax.shard_map(
        on_device,
        mesh=mesh,
        in_specs=(rows, P("leaf", None, "front"), P()),
        out_specs=(rows, rows, rows),
        check_vma=False,
    )
```

```python
import functools

import jax
import jax.numpy as jnp
from jax import lax
from jax.experimental import pallas as pl
from jax.experimental.pallas import tpu as pltpu
from jax.sharding import PartitionSpec as P

MESH = pl.DeviceIdType.MESH
HIGHEST = lax.Precision.HIGHEST
NT = (((1,), (1,)), ((), ()))
NN = (((1,), (0,)), ((), ()))
TN = (((0,), (0,)), ((), ()))
TILE = 128
SEP2_TILES = 8
f32 = jnp.float32
bf16 = jnp.bfloat16


def exact_dot(a, b, dims):
    return lax.dot_general(a, b, dims, precision=HIGHEST, preferred_element_type=f32)


def thirds(x):
    high = x.astype(bf16)
    rest = x - high.astype(f32)
    mid = rest.astype(bf16)
    low = (rest - mid.astype(f32)).astype(bf16)
    return high, mid, low


def halves(x):
    high = x.astype(bf16)
    return high, (x - high.astype(f32)).astype(bf16)


def left_stack(high, low):
    return jnp.concatenate([high, low, high], axis=1)


def right_stack(high, low):
    return jnp.concatenate([high, high, low], axis=1)


def stack_dot(left, right):
    return lax.dot_general(left, right, NT, preferred_element_type=f32)


def start_block(block, mat, tile, upper):
    row = lax.broadcasted_iota(jnp.int32, (TILE, TILE), 0)
    col = lax.broadcasted_iota(jnp.int32, (TILE, TILE), 1)
    mat[:, :TILE] = block
    mat[:, TILE:] = (row == col).astype(f32)
    tile[...] = mat[0:8, :]
    upper[...] = jnp.zeros_like(upper)


def twice(x):
    return jnp.concatenate([x, x], axis=1)


def factor_panel(step, mat, tile, upper, inv):
    base = step * 8
    sub = lax.broadcasted_iota(jnp.int32, (8, TILE), 0)
    sub_wide = lax.broadcasted_iota(jnp.int32, (8, 2 * TILE), 0)
    high, mid, low = thirds(upper[...])
    left = jnp.concatenate([high, high, mid, high, low, mid], axis=0)[:, :TILE]
    right = jnp.concatenate([high, mid, high, low, high, mid], axis=0)
    mat[...] -= lax.dot_general(left, right, TN, preferred_element_type=f32)
    rows = tile[...]
    cols = [
        jnp.take_along_axis(rows[:, :TILE], jnp.full((8, TILE), base + j, jnp.int32), axis=1) for j in range(8)
    ]
    done = []
    packed = jnp.zeros((8, 2 * TILE), f32)
    entry = {}
    for j in range(8):
        scale = lax.rsqrt(jnp.broadcast_to(cols[j][j : j + 1, :], (8, TILE)))
        column = cols[j] * scale
        for k in range(j + 1, 8):
            entry[k, j] = jnp.broadcast_to(column[k : k + 1, :], (8, TILE))
            cols[k] = cols[k] - column * entry[k, j]
        row = jnp.broadcast_to(rows[j : j + 1, :], (8, 2 * TILE))
        for p in range(j):
            row = row - twice(entry[j, p]) * done[p]
        row = row * twice(scale)
        done.append(row)
        packed = jnp.where(sub_wide == j, row, packed)
    upper[...] = packed
    inv[pl.ds(pl.multiple_of(base, 8), 8), :] = packed[:, TILE:]
    after = pl.multiple_of(jnp.minimum(base + 8, TILE - 8), 8)
    total = mat[pl.ds(after, 8), :]
    for p in range(8):
        weight = jnp.take_along_axis(done[p][:, :TILE], after + sub, axis=1)
        total = total - twice(weight) * done[p]
    tile[...] = total


PASS_ON = (
    (
        (3, (1, 0, 0)),
        (4, (0, -1, 0)), (4, (0, 1, 0)),
        (8, (1, -1, 0)), (8, (1, 1, 0)),
        (9, (0, 2, 0)),
        (12, (1, 2, 0)),
    ),
    (
        (4, (1, 0, 0)), (4, (1, 0, 1)),
        (7, (0, -1, 0)), (7, (0, 1, 0)),
        (8, (0, -1, 1)), (8, (0, 1, 1)),
        (14, (1, -1, 0)), (14, (1, 1, 0)),
        (15, (1, -1, 1)), (15, (1, 1, 1)),
        (19, (0, 2, 0)), (19, (0, 2, 1)),
        (21, (1, 2, 0)), (21, (1, 2, 1)),
    ),
)
ROW_POINT = 1


def gather_factor_kernel(
    front, weight_row,
    sibling_rows, high, low, column, top, top_inv, own_panel,
    gathered, corner_in, corner, own_rows, factors, solver, lead, inv, mat, tile, upper, weights,
    local_sem, first_send, first_recv, bulk_send, bulk_recv, row_send, row_recv,
):
    leaf = lax.axis_index("leaf")
    front_id = lax.axis_index("front")
    half = lax.rem(leaf, 2)
    chip = lax.div(front_id, 2)
    core = lax.rem(front_id, 2)
    chips = lax.div(lax.axis_size("front"), 2)
    own, other = half, 1 - half

    def chip_at(offset):
        return lax.rem(chip + offset + chips, chips)

    sibling = (leaf + 1 - 2 * half, front_id)
    right = (leaf, chip_at(1) * 2 + core)
    left = (leaf, chip_at(-1) * 2 + core)
    partner = (leaf, front_id + 1 - 2 * core)
    opposite = (leaf, chip_at(2) * 2 + core)
    sibling_right = (sibling[0], right[1])
    sibling_left = (sibling[0], left[1])
    sibling_opposite = (sibling[0], opposite[1])

    staged = []

    def stage(src, dst, condition=None):
        copy = pltpu.make_async_copy(src, dst, local_sem.at[len(staged)])
        staged.append((condition, copy))
        when(condition, copy.start)

    def when(condition, action):
        if condition is None:
            action()
        else:
            pl.when(condition)(lambda: action())

    def stage_row(r, slot, condition=None):
        rows = pl.ds(r * TILE, TILE)
        for k in range(4):
            stage(front.at[rows, pl.ds(4 * k * TILE, TILE)], slot.at[:, pl.ds(k * TILE, TILE)], condition)
        stage(front.at[rows, pl.ds(TILE, TILE)], slot.at[:, pl.ds(4 * TILE, TILE)], condition)

    corner_slot = corner_in.at[own, pl.ds(pl.multiple_of(chip * TILE, TILE), TILE)]
    for k in range(4):
        stage(front.at[pl.ds(0, TILE), pl.ds(4 * k * TILE, TILE)], corner_slot.at[:, pl.ds(k * TILE, TILE)], core == 0)
    stage_row(0, gathered.at[own, 3 * chip + 1], core == 1)
    stage_row(1, gathered.at[own, 3 * chip + 2 * core])
    for k in range(4):
        stage(front.at[:, pl.ds(4 * k * TILE, TILE)], own_rows.at[:, pl.ds(k * TILE, TILE)])

    stage(weight_row, weights)

    barrier = pltpu.get_barrier_semaphore()
    greeted = (sibling, right, left, opposite, sibling_right, sibling_left, sibling_opposite, partner)
    for device in greeted:
        pl.semaphore_signal(barrier, inc=1, device_id=device, device_id_type=MESH)
    pl.semaphore_wait(barrier, len(greeted))
    for condition, copy in staged:
        when(condition, copy.wait)

    @pl.when((core == 0) & (chip == 0) & (half == 0))
    def _():
        corner_in[0, 0:1, TILE : 2 * TILE] = weights[0:1, 0:TILE]

    sends = []

    def remote(ref, send_sem, recv_sem, device):
        return pltpu.make_async_remote_copy(
            src_ref=ref, dst_ref=ref, send_sem=send_sem, recv_sem=recv_sem, device_id=device, device_id_type=MESH
        )

    def top_pieces(child):
        refs = (corner_in.at[child, pl.ds(0, TILE), pl.ds(0, TILE)], corner_in.at[child, pl.ds(0, 8), pl.ds(TILE, TILE)])
        return [(None, ref, first_recv.at[child, 0, n]) for n, ref in enumerate(refs)]

    def first_pieces(child, offset):
        k = chip_at(offset)
        rows = pl.ds(pl.multiple_of(k * TILE, TILE), TILE)
        return (
            (k >= 1, corner_in.at[child, rows, pl.ds(0, 2 * TILE)], first_recv.at[child, k, 0]),
            (k >= 2, corner_in.at[child, rows, pl.ds(2 * TILE, 2 * TILE)], first_recv.at[child, k, 1]),
        )

    counts = {"top": 0, "pass": 16, "first": 18, 0: 0, 1: 0}

    def start(kind, pool, build, device):
        number = counts[kind]
        counts[kind] += 1

        def make():
            condition, ref, recv_sem = build()
            return condition, remote(ref, pool.at[number], recv_sem, device)

        sends.append((kind, make))
        condition, copy = make()
        when(condition, copy.start)

    def top_send_to(kind, child, devices):
        for device in devices:
            for n in range(2):
                start(kind, first_send, lambda n=n: top_pieces(child)[n], device)

    def top_arrive(child):
        for condition, ref, recv_sem in top_pieces(child):
            remote(ref, first_send.at[0], recv_sem, partner).wait_recv()

    def first_send_to(child, offset, devices, pieces=(0, 1)):
        for device in devices:
            for n in pieces:
                start("first", first_send, lambda n=n: first_pieces(child, offset)[n], device)

    def first_arrive(child, offset):
        for condition, ref, recv_sem in first_pieces(child, offset):
            when(condition, remote(ref, first_send.at[0], recv_sem, partner).wait_recv)

    def bulk_piece(child, offset, from_core, i, q):
        a = 3 * chip_at(offset) + from_core * (1 + i)
        return None, gathered.at[child, a, pl.ds(q * 64, 64)], bulk_recv.at[child, a, q]

    def bulk_send_to(kind, child, offset, i, q, devices):
        for device in devices:
            start(kind, bulk_send, lambda: bulk_piece(child, offset, kind, i, q), device)

    def bulk_arrive(child, offset, from_core, i, q):
        condition, ref, recv_sem = bulk_piece(child, offset, from_core, i, q)
        when(condition, remote(ref, bulk_send.at[0], recv_sem, partner).wait_recv)

    def bulk_step(kind, child, offset, i):
        for q in range(2):
            bulk_arrive(child, offset, kind, i, q)
            if offset == 0:
                onward = (right, left)
            elif offset == -1 and q == 0:
                onward = (right,)
            elif offset == 1 and q == 1:
                onward = (left,)
            else:
                onward = ()
            bulk_send_to(kind, child, offset, i, q, onward + (partner,))

    def own_bulk(kind):
        for i in range(1 + kind):
            for q in range(2):
                bulk_send_to(kind, own, 0, i, q, (sibling, right, left, partner))

    @pl.when((core == 0) & (chip == 0))
    def _():
        top_send_to("top", own, (sibling, right, left, opposite, sibling_right, sibling_left, sibling_opposite, partner))

    @pl.when(core == 0)
    def _():
        first_send_to(own, 0, (sibling, right, left, opposite, partner))
        own_bulk(0)
        first_arrive(other, 0)
        first_send_to(other, 0, (right, left, opposite))

        @pl.when(chip != 0)
        def _():
            top_arrive(own)
            top_send_to("pass", own, (partner,))

        top_arrive(other)
        top_send_to("first", other, (partner,))

    @pl.when(core == 1)
    def _():
        own_bulk(1)
        for child in (own, other):
            top_arrive(child)

    def pass_first():
        @pl.when(core == 0)
        def _():
            first_send_to(other, 0, (partner,))
            for child, offset in ((own, -1), (own, 1), (own, 2), (other, -1), (other, 1), (other, 2)):
                first_arrive(child, offset)
                first_send_to(child, offset, (partner,))

    def last_first():
        @pl.when(core == 1)
        def _():
            for child in (own, other):
                for offset in (0, -1, 1, 2):
                    first_arrive(child, offset)

    def row_copy(r, g):
        return pltpu.make_async_remote_copy(
            src_ref=front.at[pl.ds(r * TILE, TILE), pl.ds((4 * g + 1) * TILE, 3 * TILE)],
            dst_ref=sibling_rows.at[pl.ds(r * TILE, TILE), pl.ds(3 * g * TILE, 3 * TILE)],
            send_sem=row_send.at[r, g],
            recv_sem=row_recv.at[r, g],
            device_id=sibling,
            device_id_type=MESH,
        )

    def start_rows():
        for g in range(4):
            row_copy(1, g).start()

        @pl.when(core == 1)
        def _():
            for g in range(4):
                row_copy(0, g).start()

    def pass_on(point):
        for kind in range(2):
            listed = [step for when_, step in PASS_ON[kind] if when_ == point]
            if listed:

                @pl.when(core == kind)
                def _():
                    for sib, offset, i in listed:
                        bulk_step(kind, other if sib else own, offset, i)

    for k in range(4):
        here = slice(k * TILE, (k + 1) * TILE)
        for child in range(2):
            start_block((corner_in if k == 0 else corner)[child, here, here], mat.at[child], tile.at[child], upper.at[child])

        for part in range(4):

            @pl.loop(part * (TILE // 32), (part + 1) * (TILE // 32))
            def _(step):
                for child in range(2):
                    factor_panel(step, mat.at[child], tile.at[child], upper.at[child], inv.at[child])

            if (k, part) == (0, 1):
                pass_first()
            if (k, part) == (0, 3):
                last_first()
                corner[...] = corner_in[...]
            pass_on(4 * k + part)
            if 4 * k + part == ROW_POINT:
                start_rows()

        for child in range(2):
            finish_block(k, corner.at[child], inv.at[child], factors.at[child])

    for child in range(2):
        for j in range(3):
            solver[child, j] = right_stack(*halves(factors[child, j]))

    def solve(child, columns):
        one = stack_dot(left_stack(*halves(columns[:, : 2 * TILE])), solver[child, 0])
        one_high, one_low = halves(one)
        two = columns[:, 2 * TILE :] - stack_dot(left_stack(one_high, one_low), solver[child, 2])
        two = stack_dot(left_stack(*halves(two)), solver[child, 1])
        two_high, two_low = halves(two)
        high_low = (jnp.concatenate([one_high, two_high], axis=1), jnp.concatenate([one_low, two_low], axis=1))
        return one, two, high_low

    pass_on(16)
    one, two, _ = solve(own, own_rows[...])
    own_panel[:, : 2 * TILE] = one
    own_panel[:, 2 * TILE :] = two
    pass_on(17)

    @pl.when(core == 1)
    def _():
        for child in (own, other):
            for offset in (0, -1, 1, 2):
                for q in range(2):
                    bulk_arrive(child, offset, 0, 0, q)

    row = lax.broadcasted_iota(jnp.int32, (TILE, TILE), 0)
    col = lax.broadcasted_iota(jnp.int32, (TILE, TILE), 1)
    near = jnp.where(jnp.abs(row - col) == 1, 1.0, 0.0)
    total = jnp.where(row == col, corner_in[0, 0:1, TILE : 2 * TILE] + 4.0, 0.0) - near
    for child in range(2):
        high_low = solve(child, gathered[child, 0, :, : 4 * TILE])[2]
        lead[child] = right_stack(*high_low)
        total = total + (gathered[child, 0, :, 4 * TILE :] - stack_dot(left_stack(*high_low), lead[child]))
    top[...] = total
    start_block(total, mat.at[0], tile.at[0], upper.at[0])

    def panels(child, k):
        rows = pl.ds(3 * k, 3)
        block = gathered[child, rows].reshape(3 * TILE, 5 * TILE)
        whole_high, whole_low = solve(child, block[:, : 4 * TILE])[2]
        high[child, rows] = whole_high.reshape(3, TILE, 4 * TILE)
        low[child, rows] = whole_low.reshape(3, TILE, 4 * TILE)
        product = stack_dot(left_stack(whole_high, whole_low), lead[child])
        column[child, rows] = (block[:, 4 * TILE :] - product).reshape(3, TILE, TILE)

    def partner_rows(*groups):
        @pl.when(core == 0)
        def _():
            for child, offset in groups:
                for i in range(2):
                    for q in range(2):
                        bulk_arrive(child, offset, 1, i, q)

    pairs = (((own, 0), (other, 0)), ((own, -1), (own, 1)), ((other, -1), (other, 1)), ((own, 2), (other, 2)))

    @pl.loop(0, 4)
    def _(pair):
        for number in range(4):

            @pl.when(pair == number)
            def _():
                pass_on(18 + number)
                partner_rows(*pairs[number])

        panels(lax.select(pair == 2, other, own), chip_at(lax.select(pair == 0, 0, lax.select(pair == 3, 2, -1))))
        panels(lax.select(pair == 1, own, other), chip_at(lax.select(pair == 0, 0, lax.select(pair == 3, 2, 1))))
        for part in range(4):
            factor_panel(4 * pair + part, mat.at[0], tile.at[0], upper.at[0], top_inv)

    def sent(kind):
        for name, make in sends:
            if name == kind:
                condition, copy = make()
                when(condition, copy.wait_send)

    @pl.when(core == 0)
    def _():
        sent("first")
        sent(0)

        @pl.when(chip == 0)
        def _():
            sent("top")

        @pl.when(chip != 0)
        def _():
            sent("pass")

    @pl.when(core == 1)
    def _():
        sent(1)

    for g in range(4):
        row_copy(1, g).wait()

    @pl.when(core == 1)
    def _():
        for g in range(4):
            row_copy(0, g).wait()


def finish_block(k, corner, inv, factors):
    here = slice(k * TILE, (k + 1) * TILE)
    inverse = inv[...]
    level, place = divmod(k, 2)
    if place == 0:
        factors[level, 0:TILE, 0:TILE] = inverse
        factors[level, 0:TILE, TILE:] = jnp.zeros((TILE, TILE), f32)
    else:
        before = slice((k - 1) * TILE, k * TILE)
        middle = exact_dot(corner[here, before], factors[level, 0:TILE, 0:TILE], NN)
        factors[level, TILE:, 0:TILE] = -exact_dot(inverse, middle, NN)
        factors[level, TILE:, TILE:] = inverse
    if k < 3:
        rest = slice((k + 1) * TILE, 4 * TILE)
        below = exact_dot(corner[rest, here], inverse, NT)
        corner[rest, here] = below
        corner[rest, rest] -= exact_dot(below, below, NT)
        if level == 0:
            cut = (1 - place) * TILE
            factors[2, :, place * TILE : (place + 1) * TILE] = below[cut:, :]


def gather_factor(front, weights):
    rows, width = front.shape
    local = pl.BlockSpec(memory_space=pltpu.VMEM)
    anywhere = pl.BlockSpec(memory_space=pl.ANY)
    return pl.pallas_call(
        gather_factor_kernel,
        out_shape=(
            jax.ShapeDtypeStruct((rows, 12 * TILE), f32),
            jax.ShapeDtypeStruct((2, 12, TILE, 4 * TILE), bf16),
            jax.ShapeDtypeStruct((2, 12, TILE, 4 * TILE), bf16),
            jax.ShapeDtypeStruct((2, 12, TILE, TILE), f32),
            jax.ShapeDtypeStruct((TILE, TILE), f32),
            jax.ShapeDtypeStruct((TILE, TILE), f32),
            jax.ShapeDtypeStruct((rows, 4 * TILE), f32),
        ),
        in_specs=[pl.BlockSpec(memory_space=pltpu.HBM), pl.BlockSpec(memory_space=pltpu.HBM)],
        out_specs=(anywhere, local, local, local, local, local, local),
        scratch_shapes=[
            pltpu.VMEM((2, 12, TILE, 5 * TILE), f32),
            pltpu.VMEM((2, 4 * TILE, 4 * TILE), f32),
            pltpu.VMEM((2, 4 * TILE, 4 * TILE), f32),
            pltpu.VMEM((rows, 4 * TILE), f32),
            pltpu.VMEM((2, 3, 2 * TILE, 2 * TILE), f32),
            pltpu.VMEM((2, 3, 2 * TILE, 6 * TILE), bf16),
            pltpu.VMEM((2, TILE, 12 * TILE), bf16),
            pltpu.VMEM((2, TILE, TILE), f32),
            pltpu.VMEM((2, TILE, 2 * TILE), f32),
            pltpu.VMEM((2, 8, 2 * TILE), f32),
            pltpu.VMEM((2, 8, 2 * TILE), f32),
            pltpu.VMEM((1, 2 * TILE), f32),
            pltpu.SemaphoreType.DMA((20,)),
            pltpu.SemaphoreType.DMA((60,)),
            pltpu.SemaphoreType.DMA((2, 4, 2)),
            pltpu.SemaphoreType.DMA((80,)),
            pltpu.SemaphoreType.DMA((2, 12, 2)),
            pltpu.SemaphoreType.DMA((2, 4)),
            pltpu.SemaphoreType.DMA((2, 4)),
        ],
        compiler_params=pltpu.CompilerParams(
            collective_id=0, has_side_effects=True, vmem_limit_bytes=34 * 2**20
        ),
        name="gather_factor",
    )(front, weights)


def assemble_kernel(
    index, front, sibling_rows, weight_row, high, low, column, top, top_inv, own_panel,
    leaf_panel, parent_panel, parent_update,
    own_front, sib_front, parent, parent_high, parent_low, weights, child_of, row_sem,
):
    leaf = lax.axis_index("leaf")
    front_id = lax.axis_index("front")
    half = lax.rem(leaf, 2)
    first = leaf - half
    row_loads = [
        pltpu.make_async_copy(front, own_front, row_sem.at[0]),
        pltpu.make_async_copy(sibling_rows, sib_front, row_sem.at[1]),
        pltpu.make_async_copy(weight_row, weights, row_sem.at[2]),
    ]
    for copy in row_loads:
        copy.start()
    leaf_panel[...] = own_panel[...]

    @pl.loop(0, 32)
    def _(p):
        child_of[0, p] = -1
        child_of[1, p] = -1

    for child in range(2):
        for a in range(12):
            child_of[child, index[a, 0, first + child]] = a

    row = lax.broadcasted_iota(jnp.int32, (TILE, TILE), 0)
    col = lax.broadcasted_iota(jnp.int32, (TILE, TILE), 1)
    near = jnp.where(jnp.abs(row - col) == 1, 1.0, 0.0)
    above = jnp.where((row == 0) & (col == TILE - 1), 1.0, 0.0)
    under = jnp.where((row == TILE - 1) & (col == 0), 1.0, 0.0)

    def landed(p):
        if p == 0:
            return top[...]
        total = -above if p == 1 else jnp.zeros((TILE, TILE), f32)
        for child in range(2):
            a = child_of[child, p]
            total = total + jnp.where(a >= 0, column[child, jnp.maximum(a, 0)], 0.0)
        return total

    last = right_stack(*halves(top_inv[...]))
    for q in range(8):
        block = jnp.concatenate([landed(p) for p in range(4 * q, 4 * q + 4)], axis=0)
        done = stack_dot(left_stack(*halves(block)), last)
        parent[4 * q : 4 * q + 4] = done.reshape(4, TILE, TILE)
        done_high, done_low = halves(done)
        parent_high[4 * q * TILE : 4 * (q + 1) * TILE, :] = done_high
        parent_low[4 * q * TILE : 4 * (q + 1) * TILE, :] = done_low

    place = 4 * front_id + 2 * half
    parent_panel[...] = parent[pl.ds(place, 2)].reshape(2 * TILE, TILE)
    here = pl.ds(pl.multiple_of(place * TILE, TILE), 2 * TILE)
    mine = left_stack(parent_high[here, :], parent_low[here, :])
    for start in range(TILE, 32 * TILE, 4 * TILE):
        stop = min(start + 4 * TILE, 32 * TILE)
        there = right_stack(parent_high[start:stop, :], parent_low[start:stop, :])
        parent_update[:, start - TILE : stop - TILE] = -stack_dot(mine, there)

    def columns_of(p):
        return pl.ds(pl.multiple_of((p - 1) * TILE, TILE), TILE)

    for copy in row_loads:
        copy.wait()
    for kin in range(2):
        child = half if kin == 0 else 1 - half
        source = own_front if kin == 0 else sib_front
        landing = [child_of[child, place + r] for r in range(2)]

        @pl.when((landing[0] >= 0) | (landing[1] >= 0))
        def _():
            leads = []
            source_rows = []
            for a in landing:
                tile_row = jnp.maximum(a, 0)
                leads.append(left_stack(high[child, tile_row], low[child, tile_row]))
                local = 4 * lax.div(tile_row, 3) + lax.rem(tile_row, 3) + 1 - 2 * front_id
                local = jnp.where(a >= 0, local, 0)
                source_rows.append(pl.ds(pl.multiple_of(local * TILE, TILE), TILE))
            lead = jnp.concatenate(leads, axis=0)
            for g in range(4):
                others = right_stack(
                    high[child, pl.ds(3 * g, 3)].reshape(3 * TILE, 4 * TILE),
                    low[child, pl.ds(3 * g, 3)].reshape(3 * TILE, 4 * TILE),
                )
                product = stack_dot(lead, others)
                for m in range(3):
                    b = 3 * g + m
                    if b == 0:
                        continue
                    p = index[b, 0, first + child]
                    t = 4 * g + m + 1 if kin == 0 else b
                    for r in range(2):
                        rows = slice(r * TILE, (r + 1) * TILE)
                        value = source[source_rows[r], t * TILE : (t + 1) * TILE] - product[rows, m * TILE : (m + 1) * TILE]
                        parent_update[rows, columns_of(p)] += jnp.where(landing[r] >= 0, value, 0.0)

    for r in range(2):
        p = place + r
        rows = slice(r * TILE, (r + 1) * TILE)
        own_weights = weights[0:1, r * TILE : (r + 1) * TILE]
        inside = p < SEP2_TILES

        @pl.when(p >= 1)
        def _():
            extra = jnp.where(inside, 1.0, 0.0)
            parent_update[rows, columns_of(p)] += jnp.where(row == col, own_weights + 4.0 * extra, 0.0) - near * extra

        @pl.when((p >= 2) & inside)
        def _():
            parent_update[rows, columns_of(p - 1)] -= above

        @pl.when(p + 1 < SEP2_TILES)
        def _():
            parent_update[rows, columns_of(p + 1)] -= under


def assemble(index, front, weights, sibling_rows, *rest):
    rows, width = front.shape
    anywhere = pl.BlockSpec(memory_space=pl.ANY)
    local = pl.BlockSpec(memory_space=pltpu.VMEM)
    return pl.pallas_call(
        assemble_kernel,
        out_shape=(
            jax.ShapeDtypeStruct((rows, 4 * TILE), f32),
            jax.ShapeDtypeStruct((rows, TILE), f32),
            jax.ShapeDtypeStruct((rows, 31 * TILE), f32),
        ),
        in_specs=[pl.BlockSpec(memory_space=pltpu.SMEM), pl.BlockSpec(memory_space=pltpu.HBM), anywhere]
        + [pl.BlockSpec(memory_space=pltpu.HBM)]
        + [local] * 6,
        out_specs=(local, local, local),
        scratch_shapes=[
            pltpu.VMEM((rows, width), f32),
            pltpu.VMEM((rows, 12 * TILE), f32),
            pltpu.VMEM((32, TILE, TILE), f32),
            pltpu.VMEM((32 * TILE, TILE), bf16),
            pltpu.VMEM((32 * TILE, TILE), bf16),
            pltpu.VMEM((1, 2 * TILE), f32),
            pltpu.SMEM((2, 32), jnp.int32),
            pltpu.SemaphoreType.DMA((3,)),
        ],
        compiler_params=pltpu.CompilerParams(vmem_limit_bytes=30 * 2**20),
        name="assemble",
    )(index, front, sibling_rows, weights, *rest)


def on_device(leaf_fronts, screen_weights, parent_tile_index):
    front = leaf_fronts[0, 0]
    weights = screen_weights[0]
    index = parent_tile_index.transpose(2, 1, 0)
    front = pltpu.with_memory_space_constraint(front, pltpu.HBM)
    weights = pltpu.with_memory_space_constraint(weights, pltpu.HBM)
    leaf_panel, parent_panel, parent_update = assemble(index, front, weights, *gather_factor(front, weights))
    return leaf_panel[None, None], parent_panel[None, None], parent_update[None, None]


def solution(mesh):
    rows = P("leaf", None, "front", None)
    return jax.shard_map(
        on_device,
        mesh=mesh,
        in_specs=(rows, P("leaf", None, "front"), P()),
        out_specs=(rows, rows, rows),
        check_vma=False,
    )
```

```python
import functools

import jax
import jax.numpy as jnp
from jax import lax
from jax.experimental import pallas as pl
from jax.experimental.pallas import tpu as pltpu
from jax.sharding import PartitionSpec as P

MESH = pl.DeviceIdType.MESH
HIGHEST = lax.Precision.HIGHEST
NT = (((1,), (1,)), ((), ()))
NN = (((1,), (0,)), ((), ()))
TN = (((0,), (0,)), ((), ()))
TILE = 128
SEP2_TILES = 8
f32 = jnp.float32
bf16 = jnp.bfloat16


def exact_dot(a, b, dims):
    return lax.dot_general(a, b, dims, precision=HIGHEST, preferred_element_type=f32)


def thirds(x):
    high = x.astype(bf16)
    rest = x - high.astype(f32)
    mid = rest.astype(bf16)
    low = (rest - mid.astype(f32)).astype(bf16)
    return high, mid, low


def halves(x):
    high = x.astype(bf16)
    return high, (x - high.astype(f32)).astype(bf16)


def left_stack(high, low):
    return jnp.concatenate([high, low, high], axis=1)


def right_stack(high, low):
    return jnp.concatenate([high, high, low], axis=1)


def stack_dot(left, right):
    return lax.dot_general(left, right, NT, preferred_element_type=f32)


def start_block(block, mat, tile, upper):
    row = lax.broadcasted_iota(jnp.int32, (TILE, TILE), 0)
    col = lax.broadcasted_iota(jnp.int32, (TILE, TILE), 1)
    mat[:, :TILE] = block
    mat[:, TILE:] = (row == col).astype(f32)
    tile[...] = mat[0:8, :]
    upper[...] = jnp.zeros_like(upper)


def twice(x):
    return jnp.concatenate([x, x], axis=1)


def factor_panel(step, mat, tile, upper, inv):
    base = step * 8
    sub = lax.broadcasted_iota(jnp.int32, (8, TILE), 0)
    sub_wide = lax.broadcasted_iota(jnp.int32, (8, 2 * TILE), 0)
    high, mid, low = thirds(upper[...])
    left = jnp.concatenate([high, high, mid, high, low, mid], axis=0)[:, :TILE]
    right = jnp.concatenate([high, mid, high, low, high, mid], axis=0)
    mat[...] -= lax.dot_general(left, right, TN, preferred_element_type=f32)
    rows = tile[...]
    cols = [
        jnp.take_along_axis(rows[:, :TILE], jnp.full((8, TILE), base + j, jnp.int32), axis=1) for j in range(8)
    ]
    done = []
    packed = jnp.zeros((8, 2 * TILE), f32)
    entry = {}
    for j in range(8):
        scale = lax.rsqrt(jnp.broadcast_to(cols[j][j : j + 1, :], (8, TILE)))
        column = cols[j] * scale
        for k in range(j + 1, 8):
            entry[k, j] = jnp.broadcast_to(column[k : k + 1, :], (8, TILE))
            cols[k] = cols[k] - column * entry[k, j]
        row = jnp.broadcast_to(rows[j : j + 1, :], (8, 2 * TILE))
        for p in range(j):
            row = row - twice(entry[j, p]) * done[p]
        row = row * twice(scale)
        done.append(row)
        packed = jnp.where(sub_wide == j, row, packed)
    upper[...] = packed
    inv[pl.ds(pl.multiple_of(base, 8), 8), :] = packed[:, TILE:]
    after = pl.multiple_of(jnp.minimum(base + 8, TILE - 8), 8)
    total = mat[pl.ds(after, 8), :]
    for p in range(8):
        weight = jnp.take_along_axis(done[p][:, :TILE], after + sub, axis=1)
        total = total - twice(weight) * done[p]
    tile[...] = total


PASS_ON = (
    (
        (3, (1, 0, 0)),
        (4, (0, -1, 0)), (4, (0, 1, 0)),
        (8, (1, -1, 0)), (8, (1, 1, 0)),
        (9, (0, 2, 0)),
        (12, (1, 2, 0)),
    ),
    (
        (4, (1, 0, 0)), (4, (1, 0, 1)),
        (7, (0, -1, 0)), (7, (0, 1, 0)),
        (8, (0, -1, 1)), (8, (0, 1, 1)),
        (14, (1, -1, 0)), (14, (1, 1, 0)),
        (15, (1, -1, 1)), (15, (1, 1, 1)),
        (19, (0, 2, 0)), (19, (0, 2, 1)),
        (21, (1, 2, 0)), (21, (1, 2, 1)),
    ),
)
ROW_POINT = 1


def gather_factor_kernel(
    front, weight_row,
    sibling_rows, high, low, column, top, top_inv, own_panel,
    gathered, corner_in, corner, own_rows, factors, solver, lead, inv, mat, tile, upper, weights,
    local_sem, first_send, first_recv, bulk_send, bulk_recv, row_send, row_recv,
):
    leaf = lax.axis_index("leaf")
    front_id = lax.axis_index("front")
    half = lax.rem(leaf, 2)
    chip = lax.div(front_id, 2)
    core = lax.rem(front_id, 2)
    chips = lax.div(lax.axis_size("front"), 2)
    own, other = half, 1 - half

    def chip_at(offset):
        return lax.rem(chip + offset + chips, chips)

    sibling = (leaf + 1 - 2 * half, front_id)
    right = (leaf, chip_at(1) * 2 + core)
    left = (leaf, chip_at(-1) * 2 + core)
    partner = (leaf, front_id + 1 - 2 * core)
    opposite = (leaf, chip_at(2) * 2 + core)
    sibling_right = (sibling[0], right[1])
    sibling_left = (sibling[0], left[1])
    sibling_opposite = (sibling[0], opposite[1])

    staged = []

    def stage(src, dst, condition=None):
        copy = pltpu.make_async_copy(src, dst, local_sem.at[len(staged)])
        staged.append((condition, copy))
        when(condition, copy.start)

    def when(condition, action):
        if condition is None:
            action()
        else:
            pl.when(condition)(lambda: action())

    def stage_row(r, slot, condition=None):
        rows = pl.ds(r * TILE, TILE)
        for k in range(4):
            stage(front.at[rows, pl.ds(4 * k * TILE, TILE)], slot.at[:, pl.ds(k * TILE, TILE)], condition)
        stage(front.at[rows, pl.ds(TILE, TILE)], slot.at[:, pl.ds(4 * TILE, TILE)], condition)

    corner_slot = corner_in.at[own, pl.ds(pl.multiple_of(chip * TILE, TILE), TILE)]
    for k in range(4):
        stage(front.at[pl.ds(0, TILE), pl.ds(4 * k * TILE, TILE)], corner_slot.at[:, pl.ds(k * TILE, TILE)], core == 0)
    stage_row(0, gathered.at[own, 3 * chip + 1], core == 1)
    stage_row(1, gathered.at[own, 3 * chip + 2 * core])

    stage(weight_row, weights)
    needed_first = len(staged)
    for k in range(4):
        stage(front.at[:, pl.ds(4 * k * TILE, TILE)], own_rows.at[:, pl.ds(k * TILE, TILE)])

    barrier = pltpu.get_barrier_semaphore()
    greeted = (sibling, right, left, opposite, sibling_right, sibling_left, sibling_opposite, partner)
    for device in greeted:
        pl.semaphore_signal(barrier, inc=1, device_id=device, device_id_type=MESH)
    pl.semaphore_wait(barrier, len(greeted))
    for condition, copy in staged[:needed_first]:
        when(condition, copy.wait)

    @pl.when((core == 0) & (chip == 0) & (half == 0))
    def _():
        corner_in[0, 0:1, TILE : 2 * TILE] = weights[0:1, 0:TILE]

    sends = []

    def remote(ref, send_sem, recv_sem, device):
        return pltpu.make_async_remote_copy(
            src_ref=ref, dst_ref=ref, send_sem=send_sem, recv_sem=recv_sem, device_id=device, device_id_type=MESH
        )

    def top_pieces(child):
        refs = (corner_in.at[child, pl.ds(0, TILE), pl.ds(0, TILE)], corner_in.at[child, pl.ds(0, 8), pl.ds(TILE, TILE)])
        return [(None, ref, first_recv.at[child, 0, n]) for n, ref in enumerate(refs)]

    def first_pieces(child, offset):
        k = chip_at(offset)
        rows = pl.ds(pl.multiple_of(k * TILE, TILE), TILE)
        return (
            (k >= 1, corner_in.at[child, rows, pl.ds(0, 2 * TILE)], first_recv.at[child, k, 0]),
            (k >= 2, corner_in.at[child, rows, pl.ds(2 * TILE, 2 * TILE)], first_recv.at[child, k, 1]),
        )

    counts = {"top": 0, "pass": 16, "first": 18, 0: 0, 1: 0}

    def start(kind, pool, build, device):
        number = counts[kind]
        counts[kind] += 1

        def make():
            condition, ref, recv_sem = build()
            return condition, remote(ref, pool.at[number], recv_sem, device)

        sends.append((kind, make))
        condition, copy = make()
        when(condition, copy.start)

    def top_send_to(kind, child, devices):
        for device in devices:
            for n in range(2):
                start(kind, first_send, lambda n=n: top_pieces(child)[n], device)

    def top_arrive(child):
        for condition, ref, recv_sem in top_pieces(child):
            remote(ref, first_send.at[0], recv_sem, partner).wait_recv()

    def first_send_to(child, offset, devices, pieces=(0, 1)):
        for device in devices:
            for n in pieces:
                start("first", first_send, lambda n=n: first_pieces(child, offset)[n], device)

    def first_arrive(child, offset):
        for condition, ref, recv_sem in first_pieces(child, offset):
            when(condition, remote(ref, first_send.at[0], recv_sem, partner).wait_recv)

    def bulk_piece(child, offset, from_core, i, q):
        a = 3 * chip_at(offset) + from_core * (1 + i)
        return None, gathered.at[child, a, pl.ds(q * 64, 64)], bulk_recv.at[child, a, q]

    def bulk_send_to(kind, child, offset, i, q, devices):
        for device in devices:
            start(kind, bulk_send, lambda: bulk_piece(child, offset, kind, i, q), device)

    def bulk_arrive(child, offset, from_core, i, q):
        condition, ref, recv_sem = bulk_piece(child, offset, from_core, i, q)
        when(condition, remote(ref, bulk_send.at[0], recv_sem, partner).wait_recv)

    def bulk_step(kind, child, offset, i):
        for q in range(2):
            bulk_arrive(child, offset, kind, i, q)
            if offset == 0:
                onward = (right, left)
            elif offset == -1 and q == 0:
                onward = (right,)
            elif offset == 1 and q == 1:
                onward = (left,)
            else:
                onward = ()
            bulk_send_to(kind, child, offset, i, q, onward + (partner,))

    def own_bulk(kind):
        for i in range(1 + kind):
            for q in range(2):
                bulk_send_to(kind, own, 0, i, q, (sibling, right, left, partner))

    @pl.when((core == 0) & (chip == 0))
    def _():
        top_send_to("top", own, (sibling, right, left, opposite, sibling_right, sibling_left, sibling_opposite, partner))

    @pl.when(core == 0)
    def _():
        first_send_to(own, 0, (sibling, right, left, opposite, partner))
        own_bulk(0)
        first_arrive(other, 0)
        first_send_to(other, 0, (right, left, opposite))

        @pl.when(chip != 0)
        def _():
            top_arrive(own)
            top_send_to("pass", own, (partner,))

        top_arrive(other)
        top_send_to("first", other, (partner,))

    @pl.when(core == 1)
    def _():
        own_bulk(1)
        for child in (own, other):
            top_arrive(child)

    def pass_first():
        @pl.when(core == 0)
        def _():
            first_send_to(other, 0, (partner,))
            for child, offset in ((own, -1), (own, 1), (own, 2), (other, -1), (other, 1), (other, 2)):
                first_arrive(child, offset)
                first_send_to(child, offset, (partner,))

    def last_first():
        @pl.when(core == 1)
        def _():
            for child in (own, other):
                for offset in (0, -1, 1, 2):
                    first_arrive(child, offset)

    def row_copy(r, g):
        return pltpu.make_async_remote_copy(
            src_ref=front.at[pl.ds(r * TILE, TILE), pl.ds((4 * g + 1) * TILE, 3 * TILE)],
            dst_ref=sibling_rows.at[pl.ds(r * TILE, TILE), pl.ds(3 * g * TILE, 3 * TILE)],
            send_sem=row_send.at[r, g],
            recv_sem=row_recv.at[r, g],
            device_id=sibling,
            device_id_type=MESH,
        )

    def start_rows():
        for g in range(4):
            row_copy(1, g).start()

        @pl.when(core == 1)
        def _():
            for g in range(4):
                row_copy(0, g).start()

    def pass_on(point):
        for kind in range(2):
            listed = [step for when_, step in PASS_ON[kind] if when_ == point]
            if listed:

                @pl.when(core == kind)
                def _():
                    for sib, offset, i in listed:
                        bulk_step(kind, other if sib else own, offset, i)

    for k in range(4):
        here = slice(k * TILE, (k + 1) * TILE)
        for child in range(2):
            start_block((corner_in if k == 0 else corner)[child, here, here], mat.at[child], tile.at[child], upper.at[child])

        for part in range(4):

            @pl.loop(part * (TILE // 32), (part + 1) * (TILE // 32))
            def _(step):
                for child in range(2):
                    factor_panel(step, mat.at[child], tile.at[child], upper.at[child], inv.at[child])

            if (k, part) == (0, 1):
                pass_first()
            if (k, part) == (0, 3):
                last_first()
                corner[...] = corner_in[...]
            pass_on(4 * k + part)
            if 4 * k + part == ROW_POINT:
                start_rows()

        for child in range(2):
            finish_block(k, corner.at[child], inv.at[child], factors.at[child])

    for child in range(2):
        for j in range(3):
            solver[child, j] = right_stack(*halves(factors[child, j]))

    def solve(child, columns):
        one = stack_dot(left_stack(*halves(columns[:, : 2 * TILE])), solver[child, 0])
        one_high, one_low = halves(one)
        two = columns[:, 2 * TILE :] - stack_dot(left_stack(one_high, one_low), solver[child, 2])
        two = stack_dot(left_stack(*halves(two)), solver[child, 1])
        two_high, two_low = halves(two)
        high_low = (jnp.concatenate([one_high, two_high], axis=1), jnp.concatenate([one_low, two_low], axis=1))
        return one, two, high_low

    pass_on(16)
    for condition, copy in staged[needed_first:]:
        when(condition, copy.wait)
    one, two, _ = solve(own, own_rows[...])
    own_panel[:, : 2 * TILE] = one
    own_panel[:, 2 * TILE :] = two
    pass_on(17)

    @pl.when(core == 1)
    def _():
        for child in (own, other):
            for offset in (0, -1, 1, 2):
                for q in range(2):
                    bulk_arrive(child, offset, 0, 0, q)

    row = lax.broadcasted_iota(jnp.int32, (TILE, TILE), 0)
    col = lax.broadcasted_iota(jnp.int32, (TILE, TILE), 1)
    near = jnp.where(jnp.abs(row - col) == 1, 1.0, 0.0)
    total = jnp.where(row == col, corner_in[0, 0:1, TILE : 2 * TILE] + 4.0, 0.0) - near
    for child in range(2):
        high_low = solve(child, gathered[child, 0, :, : 4 * TILE])[2]
        lead[child] = right_stack(*high_low)
        total = total + (gathered[child, 0, :, 4 * TILE :] - stack_dot(left_stack(*high_low), lead[child]))
    top[...] = total
    start_block(total, mat.at[0], tile.at[0], upper.at[0])

    def panels(child, k):
        rows = pl.ds(3 * k, 3)
        block = gathered[child, rows].reshape(3 * TILE, 5 * TILE)
        whole_high, whole_low = solve(child, block[:, : 4 * TILE])[2]
        high[child, rows] = whole_high.reshape(3, TILE, 4 * TILE)
        low[child, rows] = whole_low.reshape(3, TILE, 4 * TILE)
        product = stack_dot(left_stack(whole_high, whole_low), lead[child])
        column[child, rows] = (block[:, 4 * TILE :] - product).reshape(3, TILE, TILE)

    def partner_rows(*groups):
        @pl.when(core == 0)
        def _():
            for child, offset in groups:
                for i in range(2):
                    for q in range(2):
                        bulk_arrive(child, offset, 1, i, q)

    pairs = (((own, 0), (other, 0)), ((own, -1), (own, 1)), ((other, -1), (other, 1)), ((own, 2), (other, 2)))

    @pl.loop(0, 4)
    def _(pair):
        for number in range(4):

            @pl.when(pair == number)
            def _():
                pass_on(18 + number)
                partner_rows(*pairs[number])

        panels(lax.select(pair == 2, other, own), chip_at(lax.select(pair == 0, 0, lax.select(pair == 3, 2, -1))))
        panels(lax.select(pair == 1, own, other), chip_at(lax.select(pair == 0, 0, lax.select(pair == 3, 2, 1))))
        for part in range(4):
            factor_panel(4 * pair + part, mat.at[0], tile.at[0], upper.at[0], top_inv)

    def sent(kind):
        for name, make in sends:
            if name == kind:
                condition, copy = make()
                when(condition, copy.wait_send)

    @pl.when(core == 0)
    def _():
        sent("first")
        sent(0)

        @pl.when(chip == 0)
        def _():
            sent("top")

        @pl.when(chip != 0)
        def _():
            sent("pass")

    @pl.when(core == 1)
    def _():
        sent(1)

    for g in range(4):
        row_copy(1, g).wait()

    @pl.when(core == 1)
    def _():
        for g in range(4):
            row_copy(0, g).wait()


def finish_block(k, corner, inv, factors):
    here = slice(k * TILE, (k + 1) * TILE)
    inverse = inv[...]
    level, place = divmod(k, 2)
    if place == 0:
        factors[level, 0:TILE, 0:TILE] = inverse
        factors[level, 0:TILE, TILE:] = jnp.zeros((TILE, TILE), f32)
    else:
        before = slice((k - 1) * TILE, k * TILE)
        middle = exact_dot(corner[here, before], factors[level, 0:TILE, 0:TILE], NN)
        factors[level, TILE:, 0:TILE] = -exact_dot(inverse, middle, NN)
        factors[level, TILE:, TILE:] = inverse
    if k < 3:
        rest = slice((k + 1) * TILE, 4 * TILE)
        below = exact_dot(corner[rest, here], inverse, NT)
        corner[rest, here] = below
        corner[rest, rest] -= exact_dot(below, below, NT)
        if level == 0:
            cut = (1 - place) * TILE
            factors[2, :, place * TILE : (place + 1) * TILE] = below[cut:, :]


def gather_factor(front, weights):
    rows, width = front.shape
    local = pl.BlockSpec(memory_space=pltpu.VMEM)
    anywhere = pl.BlockSpec(memory_space=pl.ANY)
    return pl.pallas_call(
        gather_factor_kernel,
        out_shape=(
            jax.ShapeDtypeStruct((rows, 12 * TILE), f32),
            jax.ShapeDtypeStruct((2, 12, TILE, 4 * TILE), bf16),
            jax.ShapeDtypeStruct((2, 12, TILE, 4 * TILE), bf16),
            jax.ShapeDtypeStruct((2, 12, TILE, TILE), f32),
            jax.ShapeDtypeStruct((TILE, TILE), f32),
            jax.ShapeDtypeStruct((TILE, TILE), f32),
            jax.ShapeDtypeStruct((rows, 4 * TILE), f32),
        ),
        in_specs=[pl.BlockSpec(memory_space=pltpu.HBM), pl.BlockSpec(memory_space=pltpu.HBM)],
        out_specs=(anywhere, local, local, local, local, local, local),
        scratch_shapes=[
            pltpu.VMEM((2, 12, TILE, 5 * TILE), f32),
            pltpu.VMEM((2, 4 * TILE, 4 * TILE), f32),
            pltpu.VMEM((2, 4 * TILE, 4 * TILE), f32),
            pltpu.VMEM((rows, 4 * TILE), f32),
            pltpu.VMEM((2, 3, 2 * TILE, 2 * TILE), f32),
            pltpu.VMEM((2, 3, 2 * TILE, 6 * TILE), bf16),
            pltpu.VMEM((2, TILE, 12 * TILE), bf16),
            pltpu.VMEM((2, TILE, TILE), f32),
            pltpu.VMEM((2, TILE, 2 * TILE), f32),
            pltpu.VMEM((2, 8, 2 * TILE), f32),
            pltpu.VMEM((2, 8, 2 * TILE), f32),
            pltpu.VMEM((1, 2 * TILE), f32),
            pltpu.SemaphoreType.DMA((20,)),
            pltpu.SemaphoreType.DMA((60,)),
            pltpu.SemaphoreType.DMA((2, 4, 2)),
            pltpu.SemaphoreType.DMA((80,)),
            pltpu.SemaphoreType.DMA((2, 12, 2)),
            pltpu.SemaphoreType.DMA((2, 4)),
            pltpu.SemaphoreType.DMA((2, 4)),
        ],
        compiler_params=pltpu.CompilerParams(
            collective_id=0, has_side_effects=True, vmem_limit_bytes=34 * 2**20
        ),
        name="gather_factor",
    )(front, weights)


def assemble_kernel(
    index, front, sibling_rows, weight_row, high, low, column, top, top_inv, own_panel,
    leaf_panel, parent_panel, parent_update,
    own_front, sib_front, parent, parent_high, parent_low, weights, child_of, row_sem,
):
    leaf = lax.axis_index("leaf")
    front_id = lax.axis_index("front")
    half = lax.rem(leaf, 2)
    first = leaf - half
    row_loads = [
        pltpu.make_async_copy(front, own_front, row_sem.at[0]),
        pltpu.make_async_copy(sibling_rows, sib_front, row_sem.at[1]),
        pltpu.make_async_copy(weight_row, weights, row_sem.at[2]),
    ]
    for copy in row_loads:
        copy.start()
    leaf_panel[...] = own_panel[...]

    @pl.loop(0, 32)
    def _(p):
        child_of[0, p] = -1
        child_of[1, p] = -1

    for child in range(2):
        for a in range(12):
            child_of[child, index[a, 0, first + child]] = a

    row = lax.broadcasted_iota(jnp.int32, (TILE, TILE), 0)
    col = lax.broadcasted_iota(jnp.int32, (TILE, TILE), 1)
    near = jnp.where(jnp.abs(row - col) == 1, 1.0, 0.0)
    above = jnp.where((row == 0) & (col == TILE - 1), 1.0, 0.0)
    under = jnp.where((row == TILE - 1) & (col == 0), 1.0, 0.0)

    def landed(p):
        if p == 0:
            return top[...]
        total = -above if p == 1 else jnp.zeros((TILE, TILE), f32)
        for child in range(2):
            a = child_of[child, p]
            total = total + jnp.where(a >= 0, column[child, jnp.maximum(a, 0)], 0.0)
        return total

    last = right_stack(*halves(top_inv[...]))
    for q in range(8):
        block = jnp.concatenate([landed(p) for p in range(4 * q, 4 * q + 4)], axis=0)
        done = stack_dot(left_stack(*halves(block)), last)
        parent[4 * q : 4 * q + 4] = done.reshape(4, TILE, TILE)
        done_high, done_low = halves(done)
        parent_high[4 * q * TILE : 4 * (q + 1) * TILE, :] = done_high
        parent_low[4 * q * TILE : 4 * (q + 1) * TILE, :] = done_low

    place = 4 * front_id + 2 * half
    parent_panel[...] = parent[pl.ds(place, 2)].reshape(2 * TILE, TILE)
    here = pl.ds(pl.multiple_of(place * TILE, TILE), 2 * TILE)
    mine = left_stack(parent_high[here, :], parent_low[here, :])
    for start in range(TILE, 32 * TILE, 4 * TILE):
        stop = min(start + 4 * TILE, 32 * TILE)
        there = right_stack(parent_high[start:stop, :], parent_low[start:stop, :])
        parent_update[:, start - TILE : stop - TILE] = -stack_dot(mine, there)

    def columns_of(p):
        return pl.ds(pl.multiple_of((p - 1) * TILE, TILE), TILE)

    for copy in row_loads:
        copy.wait()
    for kin in range(2):
        child = half if kin == 0 else 1 - half
        source = own_front if kin == 0 else sib_front
        landing = [child_of[child, place + r] for r in range(2)]

        @pl.when((landing[0] >= 0) | (landing[1] >= 0))
        def _():
            leads = []
            source_rows = []
            for a in landing:
                tile_row = jnp.maximum(a, 0)
                leads.append(left_stack(high[child, tile_row], low[child, tile_row]))
                local = 4 * lax.div(tile_row, 3) + lax.rem(tile_row, 3) + 1 - 2 * front_id
                local = jnp.where(a >= 0, local, 0)
                source_rows.append(pl.ds(pl.multiple_of(local * TILE, TILE), TILE))
            lead = jnp.concatenate(leads, axis=0)
            for g in range(4):
                others = right_stack(
                    high[child, pl.ds(3 * g, 3)].reshape(3 * TILE, 4 * TILE),
                    low[child, pl.ds(3 * g, 3)].reshape(3 * TILE, 4 * TILE),
                )
                product = stack_dot(lead, others)
                for m in range(3):
                    b = 3 * g + m
                    if b == 0:
                        continue
                    p = index[b, 0, first + child]
                    t = 4 * g + m + 1 if kin == 0 else b
                    for r in range(2):
                        rows = slice(r * TILE, (r + 1) * TILE)
                        value = source[source_rows[r], t * TILE : (t + 1) * TILE] - product[rows, m * TILE : (m + 1) * TILE]
                        parent_update[rows, columns_of(p)] += jnp.where(landing[r] >= 0, value, 0.0)

    for r in range(2):
        p = place + r
        rows = slice(r * TILE, (r + 1) * TILE)
        own_weights = weights[0:1, r * TILE : (r + 1) * TILE]
        inside = p < SEP2_TILES

        @pl.when(p >= 1)
        def _():
            extra = jnp.where(inside, 1.0, 0.0)
            parent_update[rows, columns_of(p)] += jnp.where(row == col, own_weights + 4.0 * extra, 0.0) - near * extra

        @pl.when((p >= 2) & inside)
        def _():
            parent_update[rows, columns_of(p - 1)] -= above

        @pl.when(p + 1 < SEP2_TILES)
        def _():
            parent_update[rows, columns_of(p + 1)] -= under


def assemble(index, front, weights, sibling_rows, *rest):
    rows, width = front.shape
    anywhere = pl.BlockSpec(memory_space=pl.ANY)
    local = pl.BlockSpec(memory_space=pltpu.VMEM)
    return pl.pallas_call(
        assemble_kernel,
        out_shape=(
            jax.ShapeDtypeStruct((rows, 4 * TILE), f32),
            jax.ShapeDtypeStruct((rows, TILE), f32),
            jax.ShapeDtypeStruct((rows, 31 * TILE), f32),
        ),
        in_specs=[pl.BlockSpec(memory_space=pltpu.SMEM), pl.BlockSpec(memory_space=pltpu.HBM), anywhere]
        + [pl.BlockSpec(memory_space=pltpu.HBM)]
        + [local] * 6,
        out_specs=(local, local, local),
        scratch_shapes=[
            pltpu.VMEM((rows, width), f32),
            pltpu.VMEM((rows, 12 * TILE), f32),
            pltpu.VMEM((32, TILE, TILE), f32),
            pltpu.VMEM((32 * TILE, TILE), bf16),
            pltpu.VMEM((32 * TILE, TILE), bf16),
            pltpu.VMEM((1, 2 * TILE), f32),
            pltpu.SMEM((2, 32), jnp.int32),
            pltpu.SemaphoreType.DMA((3,)),
        ],
        compiler_params=pltpu.CompilerParams(vmem_limit_bytes=30 * 2**20),
        name="assemble",
    )(index, front, sibling_rows, weights, *rest)


def on_device(leaf_fronts, screen_weights, parent_tile_index):
    front = leaf_fronts[0, 0]
    weights = screen_weights[0]
    index = parent_tile_index.transpose(2, 1, 0)
    front = pltpu.with_memory_space_constraint(front, pltpu.HBM)
    weights = pltpu.with_memory_space_constraint(weights, pltpu.HBM)
    leaf_panel, parent_panel, parent_update = assemble(index, front, weights, *gather_factor(front, weights))
    return leaf_panel[None, None], parent_panel[None, None], parent_update[None, None]


def solution(mesh):
    rows = P("leaf", None, "front", None)
    return jax.shard_map(
        on_device,
        mesh=mesh,
        in_specs=(rows, P("leaf", None, "front"), P()),
        out_specs=(rows, rows, rows),
        check_vma=False,
    )
```
